256 devices in a mesh: half: 2 (over core), cls: 128 (over x, y, z).
Axes of the slice: x: 4, y: 4, z: 8, core: 2. Of those that a mesh axis runs over, the one named last changes fastest.
Arguments:
- particles: bfloat16 [2, 8192, 128, 128], P('half', 'cls'), may hold values from -6 to 6
- assign: int32 [2, 8192], P('half', 'cls'), may hold values from 0 to 127, as said below
- rotation: int32 [2, 8192], P('half', 'cls'), may hold values from 0 to 35
- group: int32 [2, 8192], P('half', 'cls'), may hold values from 0 to 255
- ctf: float32 [256, 64], replicated, may hold values from -1 to 1
Outputs:
- class_avg: bfloat16 [2, 128, 128, 128], P('half', 'cls')
- residual: bfloat16 [2, 8192, 128, 128], P('half', 'cls')
- scores: bfloat16 [2, 8192, 36], P('half', 'cls')
- leverage: bfloat16 [2, 8192], P('half', 'cls')
The draws below stay inside these ranges and needn't reach their ends.
Inputs may be any that keep to these rules, and one draw needn't show every extreme that they name: `assign`: among the 64 particles of one device no class appears more than 2 times, and one class appears exactly 2 times among every device's particles.
All inputs are finite; a program needn't handle non-finite values.
Results may differ from the reference program's by a relative error of at most 0.0065.
Values may be sent and summed in bfloat16 or wider, within the bound.
No kernel may reach another device: no remote copies, remote signals or barrier semaphores. Data moves between devices by JAX's collectives and lax.ppermute only.
A program may use at most 128 MiB of HBM per device.

```python
import jax
import jax.numpy as jnp
from jax import lax

CYCLES = 64
ANGLES = 128
NROT = 36
GROUPS = 256
P_DEV = 64
K = 128
CAP = 2
PART = 8192
N_CLS = 128


def draw_assign(key, part):
    blocks = 2 * K
    slots = K * CAP
    key_hot, key_score, key_order = jax.random.split(key, 3)
    hottest = jax.random.randint(key_hot, (), 0, K)
    noise = jax.random.randint(key_score, (blocks, slots), 0, 1 << 20)
    slot_ids = jnp.arange(slots, dtype=jnp.int32)
    owner_ids = slot_ids // CAP
    ranked = jnp.where(owner_ids[None, :] == hottest, 0, noise + 1) * slots + slot_ids[None, :]
    ordered = jnp.argsort(ranked, axis=1, stable=True)
    chosen = (ordered[:, :P_DEV] // CAP).astype(jnp.int32)
    order_keys = jax.random.split(key_order, blocks)
    shuffles = jax.vmap(lambda sub: jax.random.permutation(sub, P_DEV))(order_keys)
    mixed = jnp.take_along_axis(chosen, shuffles, axis=1)
    return mixed.reshape(2, P_DEV * K).astype(jnp.int32)


def place_ends(drawn, stream_key, least, largest):
    longest = drawn.shape.index(max(drawn.shape))
    spots = []
    for shift in (0, 1):
        where = [jax.random.randint(jax.random.fold_in(stream_key, axis), (), 0, length) for axis, length in enumerate(drawn.shape)]
        where[longest] = (where[longest] + shift) % drawn.shape[longest]
        spots.append(tuple(where))
    return drawn.at[spots[0]].set(least).at[spots[1]].set(largest)


def level_of(own_key, shape, pieces, low, largest):
    loudness = 1.0
    for position, shards_of in pieces:
        draws = jax.random.uniform(jax.random.fold_in(jax.random.fold_in(own_key, 6), position), (shards_of,), jnp.float32, low / len(pieces), largest / len(pieces))
        loudness = loudness * jnp.repeat(jnp.exp(draws), shape[position] // shards_of).reshape((-1,) + (1,) * (len(shape) - 1 - position))
    return loudness


def scatter_about(stream_key, dims, spread, limit, shards=(), kind=jnp.bfloat16):
    level = level_of(stream_key, dims, shards, -0.22, 0.18) if shards else 1.0
    result = jax.random.normal(stream_key, dims, jnp.float32) * spread * level
    return jnp.minimum(jnp.maximum(result, -limit), limit).astype(kind)


def setup_inputs(seed: int = 0) -> dict:
    keys = jax.random.split(jax.random.key(seed), 6)
    return {
        "particles": scatter_about(keys[0], (2, PART, 2 * CYCLES, ANGLES), 1.0, 6.0, ((0, 2), (1, 128))),
        "assign": draw_assign(jax.random.fold_in(keys[5], 71), 0),
        "rotation": place_ends(jax.random.randint(keys[2], (2, PART), 0, NROT), jax.random.fold_in(keys[2], 1), 0, NROT - 1).astype(jnp.int32),
        "group": place_ends(jax.random.randint(keys[3], (2, PART), 0, GROUPS), jax.random.fold_in(keys[3], 1), 0, GROUPS - 1).astype(jnp.int32),
        "ctf": jnp.clip(jax.random.uniform(keys[4], (GROUPS, CYCLES), jnp.float32, -1.0, 1.0), -1.0, 1.0),
    }


wiener_tau = 1.0

def rotation_table(angles):
    turns = jnp.arange(NROT, dtype=jnp.int32)[:, None, None]
    source = jnp.arange(angles, dtype=jnp.int32)[None, :, None]
    target = jnp.arange(angles, dtype=jnp.int32)[None, None, :]
    offset = turns * angles // NROT
    fraction = (turns * angles % NROT).astype(jnp.float32) / NROT
    primary = (source == (target - offset) % angles).astype(jnp.float32)
    neighbor = (source == (target - offset - 1) % angles).astype(jnp.float32)
    return ((1.0 - fraction) * primary + fraction * neighbor).astype(jnp.bfloat16)

def cycle_weights(ctf, group_ids):
    weights = ctf[group_ids]
    return (weights, jnp.concatenate([weights, weights], axis=1))

def split_blocks(images, classes, turns, groups):
    return (images.reshape(N_CLS, P_DEV, 2 * CYCLES, ANGLES), classes.reshape(N_CLS, P_DEV), turns.reshape(N_CLS, P_DEV), groups.reshape(N_CLS, P_DEV))

def align(images, turns, table):
    return jnp.einsum('prb,pba->pra', images.astype(jnp.float32), table[turns], precision=lax.Precision.HIGHEST)

def half_sums(blocks, ctf, table):

    def step(carry, block):
        images, classes, turns, groups = block
        weights, stacked = cycle_weights(ctf, groups)
        aligned = align(images, turns, table)
        onehot = (classes[:, None] == jnp.arange(K, dtype=jnp.int32)[None, :]).astype(jnp.float32)
        weighted = (stacked[:, :, None] * aligned).reshape(images.shape[0], -1)
        class_sum = carry[0] + jnp.dot(onehot.T, weighted, precision=lax.Precision.HIGHEST)
        weight_sum = carry[1] + jnp.dot(onehot.T, weights * weights, precision=lax.Precision.HIGHEST)
        return ((class_sum, weight_sum), None)
    start = (jnp.zeros((K, 2 * CYCLES * ANGLES), jnp.float32), jnp.zeros((K, CYCLES), jnp.float32))
    (class_sum, weight_sum), _ = lax.scan(step, start, blocks)
    return (class_sum, weight_sum)

def half_outputs(blocks, ctf, table, partner_avg, weight_sum):

    def step(carry, block):
        images, classes, turns, groups = block
        weights, stacked = cycle_weights(ctf, groups)
        aligned = align(images, turns, table)
        refs = partner_avg[classes].astype(jnp.float32)
        predicted = (stacked[:, :, None] * refs).astype(jnp.bfloat16)
        residual = (aligned - predicted.astype(jnp.float32)).astype(jnp.bfloat16)
        cross = jnp.einsum('pra,prb->pab', images.astype(jnp.float32), predicted.astype(jnp.float32), precision=lax.Precision.HIGHEST)
        raw = jnp.einsum('pab,tab->pt', cross, table, precision=lax.Precision.HIGHEST)
        pixels = 2 * CYCLES * ANGLES
        first = jnp.sqrt(lax.optimization_barrier(jnp.mean(jnp.square(images.astype(jnp.float32)), axis=(1, 2))) + 1e-05)
        second = jnp.sqrt(lax.optimization_barrier(jnp.mean(jnp.square(predicted.astype(jnp.float32)), axis=(1, 2))) + 1e-05)
        scores = (raw / (jnp.sqrt(jnp.float32(pixels)) * first * second)[:, None]).astype(jnp.bfloat16)
        leverage = lax.optimization_barrier(jnp.mean(weights * weights / (weight_sum[classes] + wiener_tau), axis=1)).astype(jnp.bfloat16)
        return (carry, (residual, scores, leverage))
    _, outputs = lax.scan(step, jnp.float32(0.0), blocks)
    residual, scores, leverage = outputs
    return (residual.reshape(PART, 2 * CYCLES, ANGLES), scores.reshape(PART, NROT), leverage.reshape(PART))

def reference(particles, assign, rotation, group, ctf):
    table = rotation_table(ANGLES).astype(jnp.float32)
    averages = []
    weight_sums = []
    for which in range(2):
        blocks = split_blocks(particles[which], assign[which], rotation[which], group[which])
        class_sum, weight_sum = half_sums(blocks, ctf, table)
        denom = jnp.concatenate([weight_sum, weight_sum], axis=1)[:, :, None] + wiener_tau
        averages.append((class_sum.reshape(K, 2 * CYCLES, ANGLES) / denom).astype(jnp.bfloat16))
        weight_sums.append(weight_sum)
    residuals = []
    score_list = []
    leverages = []
    for which in range(2):
        blocks = split_blocks(particles[which], assign[which], rotation[which], group[which])
        residual, scores, leverage = half_outputs(blocks, ctf, table, averages[1 - which], weight_sums[which])
        residuals.append(residual)
        score_list.append(scores)
        leverages.append(leverage)
    return (jnp.stack(averages), jnp.stack(residuals), jnp.stack(score_list), jnp.stack(leverages))
```

```python
import math

import jax
import jax.numpy as jnp
import numpy as np
from jax import lax
from jax.experimental import pallas as pl
from jax.experimental.pallas import tpu as pltpu
from jax.sharding import PartitionSpec as P

NROT = 36
TAU = 1.0
PLANE = 16
DEPTH = 8
CLASSES = PLANE * DEPTH
ROWS = 128
LANES = 128
BAND = DEPTH * ROWS + 16
SLAB = ROWS + 16
HIGH = lax.Precision.HIGHEST
F32 = jnp.float32
BF16 = jnp.bfloat16


def rotation_steps():
    turns = np.arange(NROT)
    offset = turns * LANES // NROT
    fraction = ((turns * LANES) % NROT).astype(np.float32) / np.float32(NROT)
    keep = (np.float32(1.0) - fraction).astype(BF16).astype(np.float32)
    carry = fraction.astype(BF16).astype(np.float32)
    return offset.astype(np.int32), np.stack([keep, carry])


def lag_matrix():
    offset, parts = rotation_steps()
    out = np.zeros((LANES, LANES), np.float32)
    for r in range(NROT):
        out[offset[r] % LANES, r] += parts[0, r]
        out[(offset[r] + 1) % LANES, r] += parts[1, r]
    return out


def weights_by_shell(group_row, ctf):
    groups = ctf.shape[0]
    count = group_row.shape[1]
    pick = (lax.broadcasted_iota(jnp.int32, (groups, count), 0) == group_row).astype(F32)
    return lax.dot_general(ctf, pick, (((0,), (0,)), ((), ())), precision=HIGH, preferred_element_type=F32)


def split_pair(value):
    high = value.astype(BF16).astype(F32)
    return high, value - high


def align(image, turn, offset_ref, part_ref):
    first = pltpu.roll(image, offset_ref[turn], 1)
    second = pltpu.roll(first, 1, 1)
    return part_ref[0, turn] * first + part_ref[1, turn] * second


def sums_kernel(
    assign_ref, turn_ref, offset_ref, part_ref, images_ref, assign_row, group_row, ctf_ref, out_ref, spread, dens, slots
):
    plane = pl.program_id(0)
    count = images_ref.shape[0]
    shells = ROWS // 2

    @pl.when(plane == 0)
    def _():
        by_shell = weights_by_shell(group_row[...], ctf_ref[...])
        for i in range(count):
            spread[i] = jnp.broadcast_to(by_shell[:, i : i + 1], (shells, LANES))
        member = (lax.broadcasted_iota(jnp.int32, (CLASSES, count), 0) == assign_row[...]).astype(F32)
        square = jnp.transpose(by_shell * by_shell)
        den = lax.dot_general(member, square, (((1,), (0,)), ((), ())), precision=HIGH, preferred_element_type=F32)
        dens[...] = jnp.concatenate(split_pair(den), axis=1)

        def clear(c, _):
            slots[0, c] = -1
            slots[1, c] = -1
            return 0

        lax.fori_loop(0, CLASSES, clear, 0)

        def place(i, _):
            c = assign_ref[i]
            held = slots[0, c]
            slots[1, c] = jnp.where(held >= 0, i, -1)
            slots[0, c] = jnp.where(held >= 0, held, i)
            return 0

        lax.fori_loop(0, count, place, 0)

    def weighted(i):
        image = images_ref[i].astype(F32)
        turned = align(image, turn_ref[i], offset_ref, part_ref)
        w = spread[i]
        return jnp.concatenate([w * turned[:shells], w * turned[shells:]], axis=0)

    def one(z, _):
        c = plane * DEPTH + z
        a = slots[0, c]
        b = slots[1, c]
        at = pl.multiple_of(z * ROWS, ROWS)

        @pl.when(a < 0)
        def _():
            out_ref[0, pl.ds(at, ROWS), :] = jnp.zeros((ROWS, LANES), BF16)

        @pl.when((a >= 0) & (b < 0))
        def _():
            out_ref[0, pl.ds(at, ROWS), :] = weighted(a).astype(BF16)

        @pl.when(b >= 0)
        def _():
            out_ref[0, pl.ds(at, ROWS), :] = (weighted(a) + weighted(b)).astype(BF16)

        return 0

    lax.fori_loop(0, DEPTH, one, 0)
    tile = dens[pl.ds(pl.multiple_of(plane * DEPTH, DEPTH), DEPTH), :]
    out_ref[0, DEPTH * ROWS :, :] = jnp.concatenate([tile, jnp.zeros_like(tile)], axis=0).astype(BF16)


def class_sums(images, classes, turns, groups, ctf):
    count = images.shape[0]
    offset, parts = rotation_steps()
    return pl.pallas_call(
        sums_kernel,
        out_shape=jax.ShapeDtypeStruct((PLANE, BAND, LANES), BF16),
        grid_spec=pltpu.PrefetchScalarGridSpec(
            num_scalar_prefetch=4,
            grid=(PLANE,),
            in_specs=[
                pl.BlockSpec((count, ROWS, LANES), lambda p, *_: (0, 0, 0)),
                pl.BlockSpec((1, count), lambda p, *_: (0, 0)),
                pl.BlockSpec((1, count), lambda p, *_: (0, 0)),
                pl.BlockSpec(ctf.shape, lambda p, *_: (0, 0)),
            ],
            out_specs=pl.BlockSpec((1, BAND, LANES), lambda p, *_: (p, 0, 0)),
            scratch_shapes=[
                pltpu.VMEM((count, ROWS // 2, LANES), F32),
                pltpu.VMEM((CLASSES, LANES), F32),
                pltpu.SMEM((2, CLASSES), jnp.int32),
            ],
        ),
        compiler_params=pltpu.CompilerParams(dimension_semantics=("arbitrary",), vmem_limit_bytes=40 << 20),
        name="class_sums",
    )(classes, turns, jnp.asarray(offset), jnp.asarray(parts), images, classes[None], groups[None], ctf)


def repack_pair(pair):
    total = pair[:, : LANES // 2] + pair[:, LANES // 2 :]
    return jnp.concatenate(split_pair(total), axis=1)


def plane_kernel(band_ref, tail_ref, out_ref):
    z = pl.program_id(0)
    out_ref[0, :ROWS, :] = jnp.sum(band_ref[...].astype(F32), axis=0).astype(BF16)
    tail = repack_pair(jnp.sum(tail_ref[...].astype(F32), axis=0))
    here = lax.broadcasted_iota(jnp.int32, tail.shape, 0) == z
    row = jnp.sum(jnp.where(here, tail, 0.0), axis=0, keepdims=True)
    out_ref[0, ROWS:, :] = jnp.broadcast_to(row, (16, LANES)).astype(BF16)


def plane_sum(bands):
    return pl.pallas_call(
        plane_kernel,
        out_shape=jax.ShapeDtypeStruct((DEPTH, SLAB, LANES), BF16),
        grid=(DEPTH,),
        in_specs=[
            pl.BlockSpec((PLANE, ROWS, LANES), lambda z: (0, z, 0)),
            pl.BlockSpec((PLANE, 16, LANES), lambda z: (0, DEPTH * ROWS // 16, 0)),
        ],
        out_specs=pl.BlockSpec((1, SLAB, LANES), lambda z: (z, 0, 0)),
        compiler_params=pltpu.CompilerParams(dimension_semantics=("arbitrary",), vmem_limit_bytes=24 << 20),
        name="plane_sum",
    )(bands, bands)


def average_kernel(slab_ref, avg_ref, den_ref):
    total = jnp.sum(slab_ref[...].astype(F32), axis=0)
    pair = repack_pair(total[ROWS:])
    den_ref[...] = pair.astype(BF16)
    den = pair[:1, : LANES // 2] + pair[:1, LANES // 2 :]
    column = jnp.transpose(jnp.broadcast_to(jnp.concatenate([den, den], axis=1), (ROWS, LANES)))
    avg_ref[...] = (total[:ROWS] / (column + TAU)).astype(BF16)


def class_average(slabs):
    return pl.pallas_call(
        average_kernel,
        out_shape=(jax.ShapeDtypeStruct((ROWS, LANES), BF16), jax.ShapeDtypeStruct((16, LANES), BF16)),
        compiler_params=pltpu.CompilerParams(vmem_limit_bytes=24 << 20),
        name="class_average",
    )(slabs)


def copies_kernel(avg_ref, den_ref, out_ref):
    out_ref[0, :ROWS, :] = avg_ref[...]
    out_ref[0, ROWS:, :] = den_ref[...]


def depth_copies(avg, den):
    return pl.pallas_call(
        copies_kernel,
        out_shape=jax.ShapeDtypeStruct((DEPTH, SLAB, LANES), BF16),
        grid=(DEPTH,),
        in_specs=[pl.BlockSpec((ROWS, LANES), lambda z: (0, 0)), pl.BlockSpec((16, LANES), lambda z: (0, 0))],
        out_specs=pl.BlockSpec((1, SLAB, LANES), lambda z: (z, 0, 0)),
        compiler_params=pltpu.CompilerParams(dimension_semantics=("arbitrary",)),
        name="depth_copies",
    )(avg, den)


def band_kernel(slab_ref, out_ref):
    rows = []
    for z in range(DEPTH):
        out_ref[0, z * ROWS : (z + 1) * ROWS, :] = slab_ref[z, :ROWS, :]
        rows.append(slab_ref[z, ROWS:, :].astype(F32)[:1])
    tile = jnp.concatenate(rows, axis=0)
    out_ref[0, DEPTH * ROWS :, :] = jnp.concatenate([tile, jnp.zeros_like(tile)], axis=0).astype(BF16)


def plane_copies(slabs):
    return pl.pallas_call(
        band_kernel,
        out_shape=jax.ShapeDtypeStruct((PLANE, BAND, LANES), BF16),
        grid=(PLANE,),
        in_specs=[pl.BlockSpec((DEPTH, SLAB, LANES), lambda p: (0, 0, 0))],
        out_specs=pl.BlockSpec((1, BAND, LANES), lambda p: (p, 0, 0)),
        compiler_params=pltpu.CompilerParams(dimension_semantics=("arbitrary",), vmem_limit_bytes=24 << 20),
        name="plane_copies",
    )(slabs)


BATCH = 8


def outputs_kernel(
    assign_ref, turn_ref, offset_ref, part_ref,
    images_ref, bands_ref, group_row, ctf_ref, lag_ref,
    resid_ref, score_ref, lever_ref,
    spread, dens, lags, powers, energies,
):
    step = pl.program_id(0)
    shells = ROWS // 2
    count = spread.shape[0]

    @pl.when(step == 0)
    def _():
        by_shell = weights_by_shell(group_row[...], ctf_ref[...])
        for i in range(count):
            spread[i] = jnp.broadcast_to(by_shell[:, i : i + 1], (shells, LANES))

    def one(j, _):
        i = step * BATCH + j
        c = assign_ref[i]
        plane = c // DEPTH
        z = c % DEPTH
        image = images_ref[j]
        wide = image.astype(F32)
        turned = align(wide, turn_ref[i], offset_ref, part_ref)
        avg = bands_ref[plane, pl.ds(pl.multiple_of(z * ROWS, ROWS), ROWS), :].astype(F32)
        w = spread[i]
        predicted = jnp.concatenate([w * avg[:shells], w * avg[shells:]], axis=0).astype(BF16)
        back = predicted.astype(F32)
        resid_ref[j] = (turned - back).astype(BF16)
        cross = lax.dot_general(image, predicted, (((0,), (0,)), ((), ())), preferred_element_type=F32)
        lag = cross[:8]
        for r in range(8, LANES, 8):
            lag = lag + pltpu.roll(cross[r : r + 8], LANES - r, 1)
        lags[pl.ds(pl.multiple_of(i * 8, 8), 8), :] = lag
        powers[pl.ds(i, 1), :] = jnp.sum(wide * wide, axis=0, keepdims=True)
        energies[pl.ds(i, 1), :] = jnp.sum(back * back, axis=0, keepdims=True)
        tile = bands_ref[plane, DEPTH * ROWS :, :].astype(F32)
        here = lax.broadcasted_iota(jnp.int32, tile.shape, 0) == z
        dens[pl.ds(i, 1), :] = jnp.sum(jnp.where(here, tile, 0.0), axis=0, keepdims=True)
        return 0

    lax.fori_loop(0, BATCH, one, 0)

    @pl.when(step == pl.num_programs(0) - 1)
    def _():
        lag = lags[pl.ds(0, count, stride=8), :]
        for r in range(1, 8):
            lag = lag + pltpu.roll(lags[pl.ds(r, count, stride=8), :], LANES - r, 1)
        raw = lax.dot_general(
            lag, lag_ref[...], (((1,), (0,)), ((), ())), precision=HIGH, preferred_element_type=F32
        )
        pixels = ROWS * LANES
        first = jnp.sqrt(jnp.sum(powers[...], axis=1, keepdims=True) / pixels + 1e-05)
        second = jnp.sqrt(jnp.sum(energies[...], axis=1, keepdims=True) / pixels + 1e-05)
        score_ref[...] = (raw / (math.sqrt(pixels) * first * second))[:, :NROT].astype(BF16)
        by_shell = weights_by_shell(group_row[...], ctf_ref[...])
        pair = dens[...]
        den = jnp.transpose(pair[:, :shells] + pair[:, shells:])
        lever_ref[...] = (jnp.sum(by_shell * by_shell / (den + TAU), axis=0, keepdims=True) / shells).astype(BF16)


def particle_outputs(images, bands, classes, turns, groups, ctf):
    count = images.shape[0]
    offset, parts = rotation_steps()
    return pl.pallas_call(
        outputs_kernel,
        out_shape=(
            jax.ShapeDtypeStruct(images.shape, BF16),
            jax.ShapeDtypeStruct((count, NROT), BF16),
            jax.ShapeDtypeStruct((1, count), BF16),
        ),
        grid_spec=pltpu.PrefetchScalarGridSpec(
            num_scalar_prefetch=4,
            grid=(count // BATCH,),
            in_specs=[
                pl.BlockSpec((BATCH, ROWS, LANES), lambda s, *_: (s, 0, 0)),
                pl.BlockSpec((PLANE, BAND, LANES), lambda s, *_: (0, 0, 0), pipeline_mode=pl.Buffered(1)),
                pl.BlockSpec((1, count), lambda s, *_: (0, 0)),
                pl.BlockSpec(ctf.shape, lambda s, *_: (0, 0)),
                pl.BlockSpec((LANES, LANES), lambda s, *_: (0, 0)),
            ],
            out_specs=[
                pl.BlockSpec((BATCH, ROWS, LANES), lambda s, *_: (s, 0, 0)),
                pl.BlockSpec((count, NROT), lambda s, *_: (0, 0)),
                pl.BlockSpec((1, count), lambda s, *_: (0, 0)),
            ],
            scratch_shapes=[
                pltpu.VMEM((count, ROWS // 2, LANES), F32),
                pltpu.VMEM((count, LANES), F32),
                pltpu.VMEM((count * 8, LANES), F32),
                pltpu.VMEM((count, LANES), F32),
                pltpu.VMEM((count, LANES), F32),
            ],
        ),
        compiler_params=pltpu.CompilerParams(dimension_semantics=("arbitrary",), vmem_limit_bytes=40 << 20),
        name="particle_outputs",
    )(
        classes, turns, jnp.asarray(offset), jnp.asarray(parts),
        images, bands, groups[None], ctf, jnp.asarray(lag_matrix()),
    )


def exchange(value, groups):
    return lax.all_to_all(value, "cls", split_axis=0, concat_axis=0, tiled=True, axis_index_groups=groups)


def chip_groups():
    ids = np.arange(CLASSES).reshape(PLANE, DEPTH)
    return ids.T.tolist(), ids.tolist()


def body(particles, assign, rotation, group, ctf):
    images = particles[0]
    classes = assign[0]
    turns = rotation[0]
    groups = group[0]
    across, along = chip_groups()
    bands = exchange(class_sums(images, classes, turns, groups, ctf), across)
    slabs = exchange(plane_sum(bands), along)
    average, weight_sum = class_average(slabs)
    partner = lax.ppermute(average, "half", [(0, 1), (1, 0)])
    slabs = exchange(depth_copies(partner, weight_sum), along)
    bands = exchange(plane_copies(slabs), across)
    residual, scores, leverage = particle_outputs(images, bands, classes, turns, groups, ctf)
    return (average[None, None], residual[None], scores[None], leverage)


def solution(mesh):
    in_specs = (
        P("half", "cls", None, None),
        P("half", "cls"),
        P("half", "cls"),
        P("half", "cls"),
        P(),
    )
    out_specs = (
        P("half", "cls", None, None),
        P("half", "cls", None, None),
        P("half", "cls", None),
        P("half", "cls"),
    )
    return jax.shard_map(body, mesh=mesh, in_specs=in_specs, out_specs=out_specs, check_vma=False)
```

```python
import math

import jax
import jax.numpy as jnp
import numpy as np
from jax import lax
from jax.experimental import pallas as pl
from jax.experimental.pallas import tpu as pltpu
from jax.sharding import PartitionSpec as P

NROT = 36
TAU = 1.0
PLANE = 16
DEPTH = 8
CLASSES = PLANE * DEPTH
LANES = 128
HALF = 64
TAIL = 16
BATCH = 8
HIGH = lax.Precision.HIGHEST
F32 = jnp.float32
BF16 = jnp.bfloat16

HBM = pl.BlockSpec(memory_space=pltpu.HBM)
VMEM = pl.BlockSpec(memory_space=pltpu.VMEM)
SMEM = pl.BlockSpec(memory_space=pltpu.SMEM)


def rotation_steps():
    turns = np.arange(NROT)
    offset = turns * LANES // NROT
    fraction = ((turns * LANES) % NROT).astype(np.float32) / np.float32(NROT)
    keep = (np.float32(1.0) - fraction).astype(BF16).astype(np.float32)
    carry = fraction.astype(BF16).astype(np.float32)
    return offset, keep, carry


def lag_matrix():
    offset, keep, carry = rotation_steps()
    out = np.zeros((LANES, LANES), np.float32)
    for r in range(NROT):
        out[offset[r] % LANES, r] += keep[r]
        out[(offset[r] + 1) % LANES, r] += carry[r]
    return out


def fill_steps(offsets, parts):
    offset, keep, carry = rotation_steps()
    for r in range(NROT):
        offsets[r] = jnp.int32(int(offset[r]))
        parts[0, r] = jnp.float32(float(keep[r]))
        parts[1, r] = jnp.float32(float(carry[r]))


def contract(left, right, dims):
    return lax.dot_general(left, right, (dims, ((), ())), precision=HIGH, preferred_element_type=F32)


def weights_by_shell(group_row, table):
    groups, count = table.shape[1], group_row.shape[1]
    pick = (lax.broadcasted_iota(jnp.int32, (groups, count), 0) == group_row).astype(F32)
    return contract(table, pick, ((1,), (0,)))


def split_pair(value):
    high = value.astype(BF16).astype(F32)
    return jnp.concatenate([high, value - high], axis=1)


def join_pair(pair):
    return pair[:, : LANES // 2] + pair[:, LANES // 2 :]


def align(image, turn, offsets, parts):
    first = pltpu.roll(image, offsets[turn], 1)
    second = pltpu.roll(first, 1, 1)
    return parts[0, turn] * first + parts[1, turn] * second


def keep_columns(by_shell, columns):
    for b in range(columns.shape[0]):
        columns[b, :, :BATCH] = by_shell[:, b * BATCH : (b + 1) * BATCH]


def begin(assign, rotation, group, table, images, chunk, places, sems):
    classes, turns, assign_row, group_row, local, rows = places
    copies = [
        pltpu.make_async_copy(images.at[:, pl.ds(chunk * HALF, HALF), :], rows, sems.at[0]),
        pltpu.make_async_copy(group, group_row, sems.at[1]),
        pltpu.make_async_copy(table, local, sems.at[2]),
        pltpu.make_async_copy(assign, assign_row, sems.at[3]),
        pltpu.make_async_copy(assign, classes, sems.at[4]),
        pltpu.make_async_copy(rotation, turns, sems.at[5]),
    ]
    for copy in copies:
        copy.start()
    return copies


def place_shapes(count, groups):
    return [
        pltpu.SMEM((1, count), jnp.int32),
        pltpu.SMEM((1, count), jnp.int32),
        pltpu.VMEM((1, count), jnp.int32),
        pltpu.VMEM((1, count), jnp.int32),
        pltpu.VMEM((HALF, groups), F32),
        pltpu.VMEM((count, HALF, LANES), BF16),
        pltpu.SMEM((NROT,), jnp.int32),
        pltpu.SMEM((2, NROT), F32),
        pltpu.VMEM((count // BATCH, HALF, LANES), F32),
        pltpu.SemaphoreType.DMA((6,)),
    ]


def sums_kernel(chunk, assign, rotation, group, table, images, out, *scratch):
    places, (offsets, parts, columns, sems) = scratch[:6], scratch[6:10]
    classes, turns, assign_row, group_row, local, rows = places
    count = rows.shape[0]
    copies = begin(assign, rotation, group, table, images, chunk, places, sems)
    fill_steps(offsets, parts)
    for plane in range(PLANE):
        out[plane, : DEPTH * HALF, :] = jnp.zeros((DEPTH * HALF, LANES), BF16)
    for copy in copies:
        copy.wait()
    by_shell = weights_by_shell(group_row[...], local[...])
    keep_columns(by_shell, columns)
    if chunk == 0:
        member = (lax.broadcasted_iota(jnp.int32, (CLASSES, count), 0) == assign_row[...]).astype(F32)
        pair = split_pair(contract(member, jnp.transpose(by_shell * by_shell), ((1,), (0,))))
        for plane in range(PLANE):
            tile = pair[plane * DEPTH : (plane + 1) * DEPTH]
            out[plane, DEPTH * HALF :, :] = jnp.concatenate([tile, jnp.zeros_like(tile)], axis=0).astype(BF16)

    def batch(b, _):
        weights = columns[b]
        for j in range(BATCH):
            i = b * BATCH + j
            c = classes[0, i]
            turned = align(rows[i].astype(F32), turns[0, i], offsets, parts)
            at = pl.ds(pl.multiple_of((c % DEPTH) * HALF, HALF), HALF)
            held = out[c // DEPTH, at, :].astype(F32)
            out[c // DEPTH, at, :] = (held + weights[:, j : j + 1] * turned).astype(BF16)
        return 0

    lax.fori_loop(0, count // BATCH, batch, 0)


def class_sums(chunk, assign, rotation, group, table, images):
    count = images.shape[0]
    band = DEPTH * HALF + (TAIL if chunk == 0 else 0)
    return pl.pallas_call(
        lambda *refs: sums_kernel(chunk, *refs),
        out_shape=jax.ShapeDtypeStruct((PLANE, band, LANES), BF16),
        in_specs=[HBM] * 5,
        out_specs=VMEM,
        scratch_shapes=place_shapes(count, table.shape[1]),
        compiler_params=pltpu.CompilerParams(vmem_limit_bytes=24 << 20),
        cost_estimate=pl.CostEstimate(flops=10**9, transcendentals=0, bytes_accessed=16 << 20),
        name="class_sums_%d" % chunk,
    )(assign, rotation, group, table, images)


def plane_kernel(tailed, here, bands, *outs):
    if tailed:
        tail = jnp.sum(bands[:, DEPTH * HALF :, :].astype(F32), axis=0)
        tail = split_pair(join_pair(tail))
    for j in range(DEPTH):
        z = (here[0] + j) % DEPTH
        at = pl.ds(pl.multiple_of(z * HALF, HALF), HALF)
        total = bands[0, at, :].astype(F32)
        for p in range(1, PLANE):
            total = total + bands[p, at, :].astype(F32)
        outs[j][:HALF, :] = total.astype(BF16)
        if tailed:
            pick = lax.broadcasted_iota(jnp.int32, tail.shape, 0) == z
            row = jnp.sum(jnp.where(pick, tail, 0.0), axis=0, keepdims=True)
            outs[j][HALF:, :] = jnp.broadcast_to(row, (TAIL, LANES)).astype(BF16)


def plane_sums(tailed, here, bands):
    slab = HALF + (TAIL if tailed else 0)
    return pl.pallas_call(
        lambda *refs: plane_kernel(tailed, *refs),
        out_shape=[jax.ShapeDtypeStruct((slab, LANES), BF16)] * DEPTH,
        in_specs=[SMEM, VMEM],
        out_specs=[VMEM] * DEPTH,
        compiler_params=pltpu.CompilerParams(vmem_limit_bytes=24 << 20),
        cost_estimate=pl.CostEstimate(flops=10**7, transcendentals=0, bytes_accessed=4 << 20),
        name="plane_sums",
    )(here, bands)


def average_rows(total, den):
    column = jnp.transpose(jnp.broadcast_to(jnp.concatenate([den, den], axis=1), (LANES, LANES)))[:HALF]
    return (total / (column + TAU)).astype(BF16)


def first_average_kernel(*refs):
    slabs, (avg, tail) = refs[:DEPTH], refs[DEPTH:]
    total = sum(s[...].astype(F32) for s in slabs)
    den = join_pair(total[HALF:])
    tail[...] = split_pair(den).astype(BF16)
    avg[...] = average_rows(total[:HALF], den[:1])


def first_average(slabs):
    return pl.pallas_call(
        first_average_kernel,
        out_shape=(jax.ShapeDtypeStruct((HALF, LANES), BF16), jax.ShapeDtypeStruct((TAIL, LANES), BF16)),
        in_specs=[VMEM] * DEPTH,
        out_specs=(VMEM, VMEM),
        name="first_average",
    )(*slabs)


def second_average_kernel(*refs):
    slabs, (tail, other, avg, packed) = refs[:DEPTH], refs[DEPTH:]
    total = sum(s[...].astype(F32) for s in slabs)
    rows = average_rows(total, join_pair(tail[...].astype(F32))[:1])
    avg[...] = rows
    packed[:HALF, :] = rows
    packed[HALF:, :] = other[...]


def second_average(slabs, tail, other):
    return pl.pallas_call(
        second_average_kernel,
        out_shape=(
            jax.ShapeDtypeStruct((HALF, LANES), BF16),
            jax.ShapeDtypeStruct((HALF + TAIL, LANES), BF16),
        ),
        in_specs=[VMEM] * (DEPTH + 2),
        out_specs=(VMEM, VMEM),
        name="second_average",
    )(*slabs, tail, other)


def copies_kernel(tailed, here, *refs):
    slabs, out = refs[:DEPTH], refs[DEPTH]
    if tailed:
        rank = lax.broadcasted_iota(jnp.int32, (TAIL, LANES), 0)
        tail = jnp.zeros((TAIL, LANES), F32)
    for j in range(DEPTH):
        z = (here[0] + DEPTH - j) % DEPTH
        at = pl.ds(pl.multiple_of(z * HALF, HALF), HALF)
        value = slabs[j][:HALF, :]
        for p in range(PLANE):
            out[p, at, :] = value
        if tailed:
            tail = jnp.where(rank == z, slabs[j][HALF:, :].astype(F32), tail)
    if tailed:
        for p in range(PLANE):
            out[p, DEPTH * HALF :, :] = tail.astype(BF16)


def plane_copies(tailed, here, slabs):
    band = DEPTH * HALF + (TAIL if tailed else 0)
    return pl.pallas_call(
        lambda *refs: copies_kernel(tailed, *refs),
        out_shape=jax.ShapeDtypeStruct((PLANE, band, LANES), BF16),
        in_specs=[SMEM] + [VMEM] * DEPTH,
        out_specs=VMEM,
        compiler_params=pltpu.CompilerParams(vmem_limit_bytes=24 << 20),
        name="plane_copies",
    )(here, *slabs)


def outputs_kernel(chunk, *refs):
    assign, rotation, group, table, images, bands = refs[:6]
    if chunk == 0:
        resid, lags, powers, energies = refs[6:10]
        scratch = refs[10:]
    else:
        lags_before, powers_before, energies_before, lag_ref, _, resid, score, lever = refs[6:14]
        scratch = refs[14:]
        dens, lags, powers, energies = scratch[12:16]
    places, (offsets, parts, columns, sems) = scratch[:6], scratch[6:10]
    held, out_sems = scratch[10:12]
    classes, turns, assign_row, group_row, local, rows = places
    count = rows.shape[0]
    copies = begin(assign, rotation, group, table, images, chunk, places, sems)
    fill_steps(offsets, parts)
    for copy in copies:
        copy.wait()
    by_shell = weights_by_shell(group_row[...], local[...])
    keep_columns(by_shell, columns)

    def leave(b):
        at = pl.ds(pl.multiple_of(b * BATCH, BATCH), BATCH)
        return pltpu.make_async_copy(held.at[at], resid.at[at, pl.ds(chunk * HALF, HALF), :], out_sems.at[b])

    def batch(b, _):
        weights = columns[b]
        for j in range(BATCH):
            i = b * BATCH + j
            c = classes[0, i]
            plane, z = c // DEPTH, c % DEPTH
            image = rows[i]
            wide = image.astype(F32)
            turned = align(wide, turns[0, i], offsets, parts)
            avg = bands[plane, pl.ds(pl.multiple_of(z * HALF, HALF), HALF), :].astype(F32)
            predicted = (weights[:, j : j + 1] * avg).astype(BF16)
            back = predicted.astype(F32)
            held[i] = (turned - back).astype(BF16)
            cross = lax.dot_general(image, predicted, (((0,), (0,)), ((), ())), preferred_element_type=F32)
            lag = cross[:8]
            for r in range(8, LANES, 8):
                lag = lag + pltpu.roll(cross[r : r + 8], LANES - r, 1)
            lags[pl.ds(pl.multiple_of(i * 8, 8), 8), :] = lag
            powers[pl.ds(i, 1), :] = jnp.sum(wide * wide, axis=0, keepdims=True)
            energies[pl.ds(i, 1), :] = jnp.sum(back * back, axis=0, keepdims=True)
            if chunk == 1:
                tile = bands[plane, DEPTH * HALF :, :].astype(F32)
                pick = lax.broadcasted_iota(jnp.int32, tile.shape, 0) == z
                dens[pl.ds(i, 1), :] = jnp.sum(jnp.where(pick, tile, 0.0), axis=0, keepdims=True)
        leave(b).start()
        return 0

    lax.fori_loop(0, count // BATCH, batch, 0)
    if chunk == 1:
        shift = jnp.zeros((count, LANES), F32)
        for r in range(8):
            at = pl.ds(r, count, stride=8)
            part = lags[at, :] + lags_before[at, :]
            shift = shift + (pltpu.roll(part, LANES - r, 1) if r else part)
        raw = contract(lag_ref[...], shift, ((0,), (1,)))
        pixels = 2 * HALF * LANES
        power = jnp.sum(jnp.transpose(powers[...] + powers_before[...]), axis=0, keepdims=True)
        energy = jnp.sum(jnp.transpose(energies[...] + energies_before[...]), axis=0, keepdims=True)
        first = jnp.sqrt(power / pixels + 1e-05)
        second = jnp.sqrt(energy / pixels + 1e-05)
        score[...] = (raw / (math.sqrt(pixels) * first * second))[:NROT].astype(BF16)
        den = jnp.transpose(join_pair(dens[...]))
        lever[...] = (jnp.sum(by_shell * by_shell / (den + TAU), axis=0, keepdims=True) / HALF).astype(BF16)

    def finish(b, _):
        leave(b).wait()
        return 0

    lax.fori_loop(0, count // BATCH, finish, 0)


def output_scratch(count, groups):
    return place_shapes(count, groups) + [
        pltpu.VMEM((count, HALF, LANES), BF16),
        pltpu.SemaphoreType.DMA((count // BATCH,)),
    ]


def first_outputs(assign, rotation, group, table, images, bands):
    count = images.shape[0]
    return pl.pallas_call(
        lambda *refs: outputs_kernel(0, *refs),
        out_shape=(
            jax.ShapeDtypeStruct(images.shape, BF16),
            jax.ShapeDtypeStruct((count * 8, LANES), F32),
            jax.ShapeDtypeStruct((count, LANES), F32),
            jax.ShapeDtypeStruct((count, LANES), F32),
        ),
        in_specs=[HBM] * 5 + [VMEM],
        out_specs=(HBM, VMEM, VMEM, VMEM),
        scratch_shapes=output_scratch(count, table.shape[1]),
        compiler_params=pltpu.CompilerParams(vmem_limit_bytes=24 << 20),
        cost_estimate=pl.CostEstimate(flops=10**9, transcendentals=0, bytes_accessed=32 << 20),
        name="outputs_0",
    )(assign, rotation, group, table, images, bands)


def second_outputs(assign, rotation, group, table, images, bands, before):
    resid, lags, powers, energies = before
    count = images.shape[0]
    rows = pltpu.VMEM((count, LANES), F32)
    return pl.pallas_call(
        lambda *refs: outputs_kernel(1, *refs),
        out_shape=(
            jax.ShapeDtypeStruct(images.shape, BF16),
            jax.ShapeDtypeStruct((NROT, count), BF16),
            jax.ShapeDtypeStruct((1, count), BF16),
        ),
        in_specs=[HBM] * 5 + [VMEM] * 5 + [HBM],
        out_specs=(HBM, VMEM, VMEM),
        scratch_shapes=output_scratch(count, table.shape[1]) + [rows, pltpu.VMEM((count * 8, LANES), F32), rows, rows],
        input_output_aliases={10: 0},
        compiler_params=pltpu.CompilerParams(vmem_limit_bytes=24 << 20),
        cost_estimate=pl.CostEstimate(flops=10**9, transcendentals=0, bytes_accessed=32 << 20),
        name="outputs_1",
    )(assign, rotation, group, table, images, bands, lags, powers, energies, jnp.asarray(lag_matrix()), resid)


def across(value):
    groups = np.arange(CLASSES).reshape(PLANE, DEPTH).T.tolist()
    return lax.all_to_all(value, "cls", split_axis=0, concat_axis=0, tiled=True, axis_index_groups=groups)


def upward(chip, steps):
    return chip // DEPTH * DEPTH + (chip + steps) % DEPTH


def gather_depth(pieces):
    return [pieces[0]] + [
        lax.ppermute(pieces[j], "cls", [(i, upward(i, j)) for i in range(CLASSES)]) for j in range(1, DEPTH)
    ]


def spread_depth(value):
    return [
        lax.ppermute(
            value,
            ("half", "cls"),
            [(h * CLASSES + i, (1 - h) * CLASSES + upward(i, j)) for h in range(2) for i in range(CLASSES)],
        )
        for j in range(DEPTH)
    ]


def body(particles, assign, rotation, group, ctf):
    common = (assign, rotation, group, ctf.T, particles[0])
    here = (lax.axis_index("cls") % DEPTH).astype(jnp.int32).reshape(1)
    bands_a = across(class_sums(0, *common))
    bands_b = across(class_sums(1, *common))
    avg_a, tail = first_average(gather_depth(plane_sums(True, here, bands_a)))
    other = lax.ppermute(tail, "half", [(0, 1), (1, 0)])
    bands_a = across(plane_copies(False, here, spread_depth(avg_a)))
    avg_b, packed = second_average(gather_depth(plane_sums(False, here, bands_b)), tail, other)
    bands_b = across(plane_copies(True, here, spread_depth(packed)))
    residual, scores, leverage = second_outputs(*common, bands_b, first_outputs(*common, bands_a))
    average = jnp.concatenate([avg_a, avg_b], axis=0)
    return (average[None, None], residual[None], scores.T[None], leverage)


def solution(mesh):
    in_specs = (
        P("half", "cls", None, None),
        P("half", "cls"),
        P("half", "cls"),
        P("half", "cls"),
        P(),
    )
    out_specs = (
        P("half", "cls", None, None),
        P("half", "cls", None, None),
        P("half", "cls", None),
        P("half", "cls"),
    )
    return jax.shard_map(body, mesh=mesh, in_specs=in_specs, out_specs=out_specs, check_vma=False)
```

```python
import math

import jax
import jax.numpy as jnp
import numpy as np
from jax import lax
from jax.experimental import pallas as pl
from jax.experimental.pallas import tpu as pltpu
from jax.sharding import PartitionSpec as P

NROT = 36
TAU = 1.0
GROUP = 32
STACK = 4
DEPTH = 2 * STACK
CLASSES = GROUP * STACK
LANES = 128
ROWS = 128
SHELLS = ROWS // 2
TAIL = 16
BAND = STACK * ROWS + TAIL
SLAB = ROWS + TAIL
BATCH = 8
HIGH = lax.Precision.HIGHEST
F32 = jnp.float32
BF16 = jnp.bfloat16

HBM = pl.BlockSpec(memory_space=pltpu.HBM)
VMEM = pl.BlockSpec(memory_space=pltpu.VMEM)


def rotation_steps():
    turns = np.arange(NROT)
    offset = turns * LANES // NROT
    fraction = ((turns * LANES) % NROT).astype(np.float32) / np.float32(NROT)
    keep = (np.float32(1.0) - fraction).astype(BF16).astype(np.float32)
    carry = fraction.astype(BF16).astype(np.float32)
    return offset, keep, carry


def lag_matrix():
    offset, keep, carry = rotation_steps()
    out = np.zeros((LANES, LANES), np.float32)
    for r in range(NROT):
        out[offset[r] % LANES, r] += keep[r]
        out[(offset[r] + 1) % LANES, r] += carry[r]
    return out


def fill_steps(offsets, parts):
    offset, keep, carry = rotation_steps()
    for r in range(NROT):
        offsets[r] = jnp.int32(int(offset[r]))
        parts[0, r] = jnp.float32(float(keep[r]))
        parts[1, r] = jnp.float32(float(carry[r]))


def contract(left, right, dims):
    return lax.dot_general(left, right, (dims, ((), ())), precision=HIGH, preferred_element_type=F32)


def weights_by_shell(group_row, table):
    groups, count = table.shape[1], group_row.shape[1]
    pick = (lax.broadcasted_iota(jnp.int32, (groups, count), 0) == group_row).astype(F32)
    return contract(table, pick, ((1,), (0,)))


def split_pair(value):
    high = value.astype(BF16).astype(F32)
    return jnp.concatenate([high, value - high], axis=1)


def join_pair(pair):
    return pair[:, : LANES // 2] + pair[:, LANES // 2 :]


def align(image, turn, offsets, parts):
    first = pltpu.roll(image, offsets[turn], 1)
    second = pltpu.roll(first, 1, 1)
    return parts[0, turn] * first + parts[1, turn] * second


def keep_columns(by_shell, columns):
    for b in range(columns.shape[0]):
        columns[b, :, :BATCH] = by_shell[:, b * BATCH : (b + 1) * BATCH]


def slot_of(c):
    return (c // DEPTH) * 2 + c % 2, (c // 2) % STACK


def begin(assign, rotation, group, table, images, places, sems):
    classes, turns, assign_row, group_row, local, rows = places
    copies = [
        pltpu.make_async_copy(images, rows, sems.at[0]),
        pltpu.make_async_copy(group, group_row, sems.at[1]),
        pltpu.make_async_copy(table, local, sems.at[2]),
        pltpu.make_async_copy(assign, assign_row, sems.at[3]),
        pltpu.make_async_copy(assign, classes, sems.at[4]),
        pltpu.make_async_copy(rotation, turns, sems.at[5]),
    ]
    for copy in copies:
        copy.start()
    return copies


def place_shapes(count, groups):
    return [
        pltpu.SMEM((1, count), jnp.int32),
        pltpu.SMEM((1, count), jnp.int32),
        pltpu.VMEM((1, count), jnp.int32),
        pltpu.VMEM((1, count), jnp.int32),
        pltpu.VMEM((SHELLS, groups), F32),
        pltpu.VMEM((count, ROWS, LANES), BF16),
        pltpu.SMEM((NROT,), jnp.int32),
        pltpu.SMEM((2, NROT), F32),
        pltpu.VMEM((count // BATCH, SHELLS, LANES), F32),
        pltpu.SemaphoreType.DMA((6,)),
    ]


def scale_rows(column, value):
    return jnp.concatenate([column * value[:SHELLS], column * value[SHELLS:]], axis=0)


def sums_kernel(assign, rotation, group, table, images, out, *scratch):
    places, (offsets, parts, columns, sems) = scratch[:6], scratch[6:10]
    classes, turns, assign_row, group_row, local, rows = places
    count = rows.shape[0]
    copies = begin(assign, rotation, group, table, images, places, sems)
    fill_steps(offsets, parts)
    for d in range(GROUP):
        out[d, : STACK * ROWS, :] = jnp.zeros((STACK * ROWS, LANES), BF16)
    for copy in copies:
        copy.wait()
    by_shell = weights_by_shell(group_row[...], local[...])
    keep_columns(by_shell, columns)
    n = lax.broadcasted_iota(jnp.int32, (CLASSES, count), 0)
    d, s = n // STACK, n % STACK
    member = ((d // 2) * DEPTH + s * 2 + d % 2 == assign_row[...]).astype(F32)
    pair = split_pair(contract(member, jnp.transpose(by_shell * by_shell), ((1,), (0,))))
    blank = jnp.zeros((TAIL - STACK, LANES), F32)
    for d in range(GROUP):
        tile = jnp.concatenate([pair[d * STACK : (d + 1) * STACK], blank], axis=0)
        out[d, STACK * ROWS :, :] = tile.astype(BF16)

    def batch(b, _):
        weights = columns[b]
        for j in range(BATCH):
            i = b * BATCH + j
            d, s = slot_of(classes[0, i])
            turned = align(rows[i].astype(F32), turns[0, i], offsets, parts)
            at = pl.ds(pl.multiple_of(s * ROWS, ROWS), ROWS)
            held = out[d, at, :].astype(F32)
            out[d, at, :] = (held + scale_rows(weights[:, j : j + 1], turned)).astype(BF16)
        return 0

    lax.fori_loop(0, count // BATCH, batch, 0)


def class_sums(assign, rotation, group, table, images):
    return pl.pallas_call(
        sums_kernel,
        out_shape=jax.ShapeDtypeStruct((GROUP, BAND, LANES), BF16),
        in_specs=[HBM] * 5,
        out_specs=VMEM,
        scratch_shapes=place_shapes(images.shape[0], table.shape[1]),
        compiler_params=pltpu.CompilerParams(vmem_limit_bytes=24 << 20),
        name="class_sums",
    )(assign, rotation, group, table, images)


def place_along_z():
    return lax.axis_index("cls") // 2 % STACK


def group_kernel(bands, *outs):
    here = place_along_z()
    tail = jnp.sum(bands[:, STACK * ROWS :, :].astype(F32), axis=0)
    tail = split_pair(join_pair(tail))
    for j in range(STACK):
        s = (here + j) % STACK
        for half in range(2):
            at = pl.ds(pl.multiple_of(s * ROWS + half * SHELLS, SHELLS), SHELLS)
            total = bands[0, at, :].astype(F32)
            for d in range(1, GROUP):
                total = total + bands[d, at, :].astype(F32)
            outs[j][half * SHELLS : (half + 1) * SHELLS, :] = total.astype(BF16)
        pick = lax.broadcasted_iota(jnp.int32, tail.shape, 0) == s
        row = jnp.sum(jnp.where(pick, tail, 0.0), axis=0, keepdims=True)
        outs[j][ROWS:, :] = jnp.broadcast_to(row, (TAIL, LANES)).astype(BF16)


def group_sums(bands):
    return pl.pallas_call(
        group_kernel,
        out_shape=[jax.ShapeDtypeStruct((SLAB, LANES), BF16)] * STACK,
        in_specs=[VMEM],
        out_specs=[VMEM] * STACK,
        compiler_params=pltpu.CompilerParams(vmem_limit_bytes=24 << 20),
        name="group_sums",
    )(bands)


def average_kernel(*refs):
    slabs, (avg, tail) = refs[:STACK], refs[STACK:]
    total = sum(s[...].astype(F32) for s in slabs)
    den = join_pair(total[ROWS:])
    tail[...] = split_pair(den).astype(BF16)
    column = jnp.transpose(jnp.broadcast_to(jnp.concatenate([den[:1], den[:1]], axis=1), (LANES, LANES)))
    avg[...] = (total[:ROWS] / (column + TAU)).astype(BF16)


def class_average(slabs):
    return pl.pallas_call(
        average_kernel,
        out_shape=(jax.ShapeDtypeStruct((ROWS, LANES), BF16), jax.ShapeDtypeStruct((TAIL, LANES), BF16)),
        in_specs=[VMEM] * STACK,
        out_specs=(VMEM, VMEM),
        name="class_average",
    )(*slabs)


def copies_kernel(*refs):
    here = place_along_z()
    slabs, out = refs[:STACK], refs[STACK]
    rank = lax.broadcasted_iota(jnp.int32, (TAIL, LANES), 0)
    tail = jnp.zeros((TAIL, LANES), F32)
    for j in range(STACK):
        s = (here + STACK - j) % STACK
        at = pl.ds(pl.multiple_of(s * ROWS, ROWS), ROWS)
        value = slabs[j][:ROWS, :]
        for d in range(GROUP):
            out[d, at, :] = value
        tail = jnp.where(rank == s, slabs[j][ROWS:, :].astype(F32), tail)
    for d in range(GROUP):
        out[d, STACK * ROWS :, :] = tail.astype(BF16)


def group_copies(slabs):
    return pl.pallas_call(
        copies_kernel,
        out_shape=jax.ShapeDtypeStruct((GROUP, BAND, LANES), BF16),
        in_specs=[VMEM] * STACK,
        out_specs=VMEM,
        compiler_params=pltpu.CompilerParams(vmem_limit_bytes=24 << 20),
        name="group_copies",
    )(*slabs)


def outputs_kernel(assign, rotation, group, table, images, bands, lag_ref, resid, score, lever, *scratch):
    places, (offsets, parts, columns, sems) = scratch[:6], scratch[6:10]
    held, out_sems, dens, lags, powers, energies = scratch[10:16]
    classes, turns, assign_row, group_row, local, rows = places
    count = rows.shape[0]
    copies = begin(assign, rotation, group, table, images, places, sems)
    fill_steps(offsets, parts)
    for copy in copies:
        copy.wait()
    by_shell = weights_by_shell(group_row[...], local[...])
    keep_columns(by_shell, columns)

    def leave(b):
        at = pl.ds(pl.multiple_of(b * BATCH, BATCH), BATCH)
        return pltpu.make_async_copy(held.at[at], resid.at[at], out_sems.at[b])

    def batch(b, _):
        weights = columns[b]
        for j in range(BATCH):
            i = b * BATCH + j
            d, s = slot_of(classes[0, i])
            image = rows[i]
            wide = image.astype(F32)
            turned = align(wide, turns[0, i], offsets, parts)
            avg = bands[d, pl.ds(pl.multiple_of(s * ROWS, ROWS), ROWS), :].astype(F32)
            predicted = scale_rows(weights[:, j : j + 1], avg).astype(BF16)
            back = predicted.astype(F32)
            held[i] = (turned - back).astype(BF16)
            cross = lax.dot_general(image, predicted, (((0,), (0,)), ((), ())), preferred_element_type=F32)
            lag = cross[:8]
            for r in range(8, LANES, 8):
                lag = lag + pltpu.roll(cross[r : r + 8], LANES - r, 1)
            lags[pl.ds(pl.multiple_of(i * 8, 8), 8), :] = lag
            powers[pl.ds(i, 1), :] = jnp.sum(wide * wide, axis=0, keepdims=True)
            energies[pl.ds(i, 1), :] = jnp.sum(back * back, axis=0, keepdims=True)
            tile = bands[d, STACK * ROWS :, :].astype(F32)
            pick = lax.broadcasted_iota(jnp.int32, tile.shape, 0) == s
            dens[pl.ds(i, 1), :] = jnp.sum(jnp.where(pick, tile, 0.0), axis=0, keepdims=True)
        leave(b).start()
        return 0

    lax.fori_loop(0, count // BATCH, batch, 0)
    shift = lags[pl.ds(0, count, stride=8), :]
    for r in range(1, 8):
        shift = shift + pltpu.roll(lags[pl.ds(r, count, stride=8), :], LANES - r, 1)
    raw = contract(lag_ref[...], shift, ((0,), (1,)))
    pixels = ROWS * LANES
    power = jnp.sum(jnp.transpose(powers[...]), axis=0, keepdims=True)
    energy = jnp.sum(jnp.transpose(energies[...]), axis=0, keepdims=True)
    first = jnp.sqrt(power / pixels + 1e-05)
    second = jnp.sqrt(energy / pixels + 1e-05)
    score[...] = (raw / (math.sqrt(pixels) * first * second))[:NROT].astype(BF16)
    den = jnp.transpose(join_pair(dens[...]))
    lever[...] = (jnp.sum(by_shell * by_shell / (den + TAU), axis=0, keepdims=True) / SHELLS).astype(BF16)

    def finish(b, _):
        leave(b).wait()
        return 0

    lax.fori_loop(0, count // BATCH, finish, 0)


def particle_outputs(assign, rotation, group, table, images, bands):
    count = images.shape[0]
    per_particle = pltpu.VMEM((count, LANES), F32)
    return pl.pallas_call(
        outputs_kernel,
        out_shape=(
            jax.ShapeDtypeStruct(images.shape, BF16),
            jax.ShapeDtypeStruct((NROT, count), BF16),
            jax.ShapeDtypeStruct((1, count), BF16),
        ),
        in_specs=[HBM] * 5 + [VMEM] * 2,
        out_specs=(HBM, VMEM, VMEM),
        scratch_shapes=place_shapes(count, table.shape[1])
        + [
            pltpu.VMEM((count, ROWS, LANES), BF16),
            pltpu.SemaphoreType.DMA((count // BATCH,)),
            per_particle,
            pltpu.VMEM((count * 8, LANES), F32),
            per_particle,
            per_particle,
        ],
        compiler_params=pltpu.CompilerParams(vmem_limit_bytes=24 << 20),
        name="particle_outputs",
    )(assign, rotation, group, table, images, bands, jnp.asarray(lag_matrix()))


def exchange(value):
    chips = np.arange(CLASSES).reshape(GROUP // 2, STACK, 2)
    groups = [chips[:, k, :].reshape(-1).tolist() for k in range(STACK)]
    return lax.all_to_all(value, "cls", split_axis=0, concat_axis=0, tiled=True, axis_index_groups=groups)


def upward(chip, steps):
    return chip // DEPTH * DEPTH + (chip + 2 * steps) % DEPTH


def shift(value, steps):
    return lax.ppermute(value, "cls", [(i, upward(i, steps)) for i in range(CLASSES)])


def body(particles, assign, rotation, group, ctf):
    common = [pltpu.with_memory_space_constraint(x, pltpu.HBM) for x in (assign, rotation, group, ctf.T, particles[0])]
    pieces = group_sums(exchange(class_sums(*common)))
    average, tail = class_average([pieces[0]] + [shift(pieces[j], j) for j in range(1, STACK)])
    partner = lax.ppermute(average, "half", [(0, 1), (1, 0)])
    packed = jnp.concatenate([partner, tail], axis=0)
    bands = exchange(group_copies([packed] + [shift(packed, j) for j in range(1, STACK)]))
    residual, scores, leverage = particle_outputs(*common, bands)
    return (average[None, None], residual[None], scores.T[None], leverage)


def solution(mesh):
    in_specs = (
        P("half", "cls", None, None),
        P("half", "cls"),
        P("half", "cls"),
        P("half", "cls"),
        P(),
    )
    out_specs = (
        P("half", "cls", None, None),
        P("half", "cls", None, None),
        P("half", "cls", None),
        P("half", "cls"),
    )
    return jax.shard_map(body, mesh=mesh, in_specs=in_specs, out_specs=out_specs, check_vma=False)
```

```python
import math

import jax
import jax.numpy as jnp
import numpy as np
from jax import lax
from jax.experimental import pallas as pl
from jax.experimental.pallas import tpu as pltpu
from jax.sharding import PartitionSpec as P

NROT = 36
TAU = 1.0
GROUP = 32
STACK = 4
DEPTH = 2 * STACK
CLASSES = GROUP * STACK
LANES = 128
ROWS = 128
SHELLS = ROWS // 2
TAIL = 16
BAND = STACK * ROWS + TAIL
SLAB = ROWS + TAIL
BATCH = 8
HIGH = lax.Precision.HIGHEST
F32 = jnp.float32
BF16 = jnp.bfloat16

HBM = pl.BlockSpec(memory_space=pltpu.HBM)
VMEM = pl.BlockSpec(memory_space=pltpu.VMEM)
SMEM = pl.BlockSpec(memory_space=pltpu.SMEM)


def rotation_steps():
    turns = np.arange(NROT)
    offset = turns * LANES // NROT
    fraction = ((turns * LANES) % NROT).astype(np.float32) / np.float32(NROT)
    keep = (np.float32(1.0) - fraction).astype(BF16).astype(np.float32)
    carry = fraction.astype(BF16).astype(np.float32)
    return offset, keep, carry


def lag_matrix():
    offset, keep, carry = rotation_steps()
    out = np.zeros((LANES, LANES), np.float32)
    for r in range(NROT):
        out[offset[r] % LANES, r] += keep[r]
        out[(offset[r] + 1) % LANES, r] += carry[r]
    return out


def rotation_matrices():
    offset, keep, carry = rotation_steps()
    out = np.zeros((NROT, LANES, LANES), np.float32)
    t = np.arange(LANES)
    for r in range(NROT):
        out[r, (t - offset[r]) % LANES, t] += keep[r]
        out[r, (t - offset[r] - 1) % LANES, t] += carry[r]
    return out.astype(BF16)


def contract(left, right, dims):
    return lax.dot_general(left, right, (dims, ((), ())), precision=HIGH, preferred_element_type=F32)


def weights_by_shell(group_row, table):
    groups, count = table.shape[1], group_row.shape[1]
    pick = (lax.broadcasted_iota(jnp.int32, (groups, count), 0) == group_row).astype(F32)
    return contract(table, pick, ((1,), (0,)))


def split_pair(value):
    high = value.astype(BF16).astype(F32)
    return jnp.concatenate([high, value - high], axis=1)


def join_pair(pair):
    return pair[:, : LANES // 2] + pair[:, LANES // 2 :]


def align(image, turn, rots):
    return jnp.dot(image, rots[turn], preferred_element_type=F32)


def keep_columns(by_shell, columns):
    for b in range(columns.shape[0]):
        columns[b, :, :BATCH] = by_shell[:, b * BATCH : (b + 1) * BATCH]


def slot_of(c):
    return (c // DEPTH) * 2 + c % 2, (c // 2) % STACK


def scale_rows(column, value):
    return jnp.concatenate([column * value[:SHELLS], column * value[SHELLS:]], axis=0)


def sums_kernel(assign, rotation, group, table, images, rotations, out, *scratch):
    classes, turns, assign_row, group_row, local, rows, rots, columns, sems = scratch
    count = rows.shape[0]
    moves = [
        (images, rows),
        (rotations, rots),
        (table, local),
        (group, group_row),
        (assign, assign_row),
        (assign, classes),
        (rotation, turns),
    ]
    copies = [pltpu.make_async_copy(source, target, sems.at[n]) for n, (source, target) in enumerate(moves)]
    for copy in copies:
        copy.start()
    for d in range(GROUP):
        out[d, : STACK * ROWS, :] = jnp.zeros((STACK * ROWS, LANES), BF16)
    for copy in copies[2:]:
        copy.wait()
    by_shell = weights_by_shell(group_row[...], local[...])
    keep_columns(by_shell, columns)
    n = lax.broadcasted_iota(jnp.int32, (CLASSES, count), 0)
    d, s = n // STACK, n % STACK
    member = ((d // 2) * DEPTH + s * 2 + d % 2 == assign_row[...]).astype(F32)
    pair = split_pair(contract(member, jnp.transpose(by_shell * by_shell), ((1,), (0,))))
    blank = jnp.zeros((TAIL - STACK, LANES), F32)
    for d in range(GROUP):
        tile = jnp.concatenate([pair[d * STACK : (d + 1) * STACK], blank], axis=0)
        out[d, STACK * ROWS :, :] = tile.astype(BF16)

    for copy in copies[:2]:
        copy.wait()

    def batch(b, _):
        weights = columns[b]
        for j in range(BATCH):
            i = b * BATCH + j
            d, s = slot_of(classes[0, i])
            turned = align(rows[i], turns[0, i], rots)
            at = pl.ds(pl.multiple_of(s * ROWS, ROWS), ROWS)
            held = out[d, at, :].astype(F32)
            out[d, at, :] = (held + scale_rows(weights[:, j : j + 1], turned)).astype(BF16)
        return 0

    lax.fori_loop(0, count // BATCH, batch, 0)


def class_sums(assign, rotation, group, table, images, rotations):
    count, groups = images.shape[0], table.shape[1]
    return pl.pallas_call(
        sums_kernel,
        out_shape=jax.ShapeDtypeStruct((GROUP, BAND, LANES), BF16),
        in_specs=[HBM] * 6,
        out_specs=VMEM,
        scratch_shapes=[
            pltpu.SMEM((1, count), jnp.int32),
            pltpu.SMEM((1, count), jnp.int32),
            pltpu.VMEM((1, count), jnp.int32),
            pltpu.VMEM((1, count), jnp.int32),
            pltpu.VMEM((SHELLS, groups), F32),
            pltpu.VMEM((count, ROWS, LANES), BF16),
            pltpu.VMEM((NROT, LANES, LANES), BF16),
            pltpu.VMEM((count // BATCH, SHELLS, LANES), F32),
            pltpu.SemaphoreType.DMA((7,)),
        ],
        compiler_params=pltpu.CompilerParams(vmem_limit_bytes=24 << 20),
        name="class_sums",
    )(assign, rotation, group, table, images, rotations)


def place_along_z():
    return lax.axis_index("cls") // 2 % STACK


def group_kernel(bands, *outs):
    here = place_along_z()
    tail = jnp.sum(bands[:, STACK * ROWS :, :].astype(F32), axis=0)
    tail = split_pair(join_pair(tail))
    for j in range(STACK):
        s = (here + j) % STACK
        for half in range(2):
            at = pl.ds(pl.multiple_of(s * ROWS + half * SHELLS, SHELLS), SHELLS)
            total = bands[0, at, :].astype(F32)
            for d in range(1, GROUP):
                total = total + bands[d, at, :].astype(F32)
            outs[j][half * SHELLS : (half + 1) * SHELLS, :] = total.astype(BF16)
        outs[j][ROWS:, :] = tail.astype(BF16)


def group_sums(bands):
    return pl.pallas_call(
        group_kernel,
        out_shape=[jax.ShapeDtypeStruct((SLAB, LANES), BF16)] * STACK,
        in_specs=[VMEM],
        out_specs=[VMEM] * STACK,
        compiler_params=pltpu.CompilerParams(vmem_limit_bytes=24 << 20),
        name="group_sums",
    )(bands)


def average_kernel(*refs):
    slabs, (avg, tail) = refs[:STACK], refs[STACK:]
    total = sum(s[...].astype(F32) for s in slabs)
    den = join_pair(total[ROWS:])
    tail[...] = split_pair(den).astype(BF16)
    here = lax.broadcasted_iota(jnp.int32, den.shape, 0) == place_along_z()
    den = jnp.sum(jnp.where(here, den, 0.0), axis=0, keepdims=True)
    column = jnp.transpose(jnp.broadcast_to(jnp.concatenate([den, den], axis=1), (LANES, LANES)))
    avg[...] = (total[:ROWS] / (column + TAU)).astype(BF16)


def class_average(slabs):
    return pl.pallas_call(
        average_kernel,
        out_shape=(jax.ShapeDtypeStruct((ROWS, LANES), BF16), jax.ShapeDtypeStruct((TAIL, LANES), BF16)),
        in_specs=[VMEM] * STACK,
        out_specs=(VMEM, VMEM),
        compiler_params=pltpu.CompilerParams(vmem_limit_bytes=4 << 20),
        name="class_average",
    )(*slabs)


def copies_kernel(tail, *refs):
    slabs, out = refs[:STACK], refs[STACK]
    here = place_along_z()
    for j in range(STACK):
        s = (here + STACK - j) % STACK
        at = pl.ds(pl.multiple_of(s * ROWS, ROWS), ROWS)
        value = slabs[j][...]
        for d in range(GROUP):
            out[d, at, :] = value
    value = tail[...]
    for d in range(GROUP):
        out[d, STACK * ROWS :, :] = value


def group_copies(tail, slabs):
    return pl.pallas_call(
        copies_kernel,
        out_shape=jax.ShapeDtypeStruct((GROUP, BAND, LANES), BF16),
        in_specs=[VMEM] * (STACK + 1),
        out_specs=VMEM,
        compiler_params=pltpu.CompilerParams(vmem_limit_bytes=24 << 20),
        name="group_copies",
    )(tail, *slabs)


def outputs_kernel(classes, turns, group_row, table, rows, rots, bands, lag_ref, resid, score, lever, *scratch):
    columns, held, out_sems, dens, lags, powers, energies = scratch
    count = rows.shape[0]
    by_shell = weights_by_shell(group_row[...], table[...])
    keep_columns(by_shell, columns)

    def leave(b):
        at = pl.ds(pl.multiple_of(b * BATCH, BATCH), BATCH)
        return pltpu.make_async_copy(held.at[at], resid.at[at], out_sems.at[b])

    def batch(b, _):
        weights = columns[b]
        for j in range(BATCH):
            i = b * BATCH + j
            d, s = slot_of(classes[0, i])
            image = rows[i]
            wide = image.astype(F32)
            turned = align(image, turns[0, i], rots)
            avg = bands[d, pl.ds(pl.multiple_of(s * ROWS, ROWS), ROWS), :].astype(F32)
            predicted = scale_rows(weights[:, j : j + 1], avg).astype(BF16)
            back = predicted.astype(F32)
            held[i] = (turned - back).astype(BF16)
            cross = lax.dot_general(image, predicted, (((0,), (0,)), ((), ())), preferred_element_type=F32)
            lag = cross[:8]
            for r in range(8, LANES, 8):
                lag = lag + pltpu.roll(cross[r : r + 8], LANES - r, 1)
            lags[pl.ds(pl.multiple_of(i * 8, 8), 8), :] = lag
            powers[pl.ds(i, 1), :] = jnp.sum(wide * wide, axis=0, keepdims=True)
            energies[pl.ds(i, 1), :] = jnp.sum(back * back, axis=0, keepdims=True)
            tile = bands[d, STACK * ROWS :, :].astype(F32)
            pick = lax.broadcasted_iota(jnp.int32, tile.shape, 0) == s
            dens[pl.ds(i, 1), :] = jnp.sum(jnp.where(pick, tile, 0.0), axis=0, keepdims=True)
        leave(b).start()
        return 0

    lax.fori_loop(0, count // BATCH, batch, 0)
    shift = lags[pl.ds(0, count, stride=8), :]
    for r in range(1, 8):
        shift = shift + pltpu.roll(lags[pl.ds(r, count, stride=8), :], LANES - r, 1)
    raw = contract(lag_ref[...], shift, ((0,), (1,)))
    pixels = ROWS * LANES
    power = jnp.sum(jnp.transpose(powers[...]), axis=0, keepdims=True)
    energy = jnp.sum(jnp.transpose(energies[...]), axis=0, keepdims=True)
    first = jnp.sqrt(power / pixels + 1e-05)
    second = jnp.sqrt(energy / pixels + 1e-05)
    score[...] = (raw / (math.sqrt(pixels) * first * second))[:NROT].astype(BF16)
    den = jnp.transpose(join_pair(dens[...]))
    lever[...] = (jnp.sum(by_shell * by_shell / (den + TAU), axis=0, keepdims=True) / SHELLS).astype(BF16)

    def finish(b, _):
        leave(b).wait()
        return 0

    lax.fori_loop(0, count // BATCH, finish, 0)


def particle_outputs(assign, rotation, group, table, images, rotations, bands):
    count = images.shape[0]
    per_particle = pltpu.VMEM((count, LANES), F32)
    return pl.pallas_call(
        outputs_kernel,
        out_shape=(
            jax.ShapeDtypeStruct(images.shape, BF16),
            jax.ShapeDtypeStruct((NROT, count), BF16),
            jax.ShapeDtypeStruct((1, count), BF16),
        ),
        in_specs=[SMEM] * 2 + [VMEM] * 6,
        out_specs=(HBM, VMEM, VMEM),
        scratch_shapes=[
            pltpu.VMEM((count // BATCH, SHELLS, LANES), F32),
            pltpu.VMEM((count, ROWS, LANES), BF16),
            pltpu.SemaphoreType.DMA((count // BATCH,)),
            per_particle,
            pltpu.VMEM((count * 8, LANES), F32),
            per_particle,
            per_particle,
        ],
        compiler_params=pltpu.CompilerParams(vmem_limit_bytes=24 << 20),
        name="particle_outputs",
    )(assign, rotation, group, table, images, rotations, bands, jnp.asarray(lag_matrix()))


def exchange(value):
    chips = np.arange(CLASSES).reshape(GROUP // 2, STACK, 2)
    groups = [chips[:, k, :].reshape(-1).tolist() for k in range(STACK)]
    return lax.all_to_all(value, "cls", split_axis=0, concat_axis=0, tiled=True, axis_index_groups=groups)


def upward(chip, steps):
    return chip // DEPTH * DEPTH + (chip + 2 * steps) % DEPTH


def shift(value, steps):
    return lax.ppermute(value, "cls", [(i, upward(i, steps)) for i in range(CLASSES)])


def cross(value, steps):
    pairs = [(h * CLASSES + i, (1 - h) * CLASSES + upward(i, steps)) for h in range(2) for i in range(CLASSES)]
    return lax.ppermute(value, ("half", "cls"), pairs)


def body(particles, assign, rotation, group, ctf):
    operands = (assign, rotation, group, ctf.T, particles[0], jnp.asarray(rotation_matrices()))
    pinned = [pltpu.with_memory_space_constraint(x, pltpu.HBM) for x in operands]
    pieces = group_sums(exchange(class_sums(*pinned)))
    average, tail = class_average([pieces[0]] + [shift(pieces[j], j) for j in range(1, STACK)])
    bands = exchange(group_copies(tail, [cross(average, j) for j in range(STACK)]))
    residual, scores, leverage = particle_outputs(*operands, bands)
    return (average[None, None], residual[None], scores.T[None], leverage)


def solution(mesh):
    in_specs = (
        P("half", "cls", None, None),
        P("half", "cls"),
        P("half", "cls"),
        P("half", "cls"),
        P(),
    )
    out_specs = (
        P("half", "cls", None, None),
        P("half", "cls", None, None),
        P("half", "cls", None),
        P("half", "cls"),
    )
    return jax.shard_map(body, mesh=mesh, in_specs=in_specs, out_specs=out_specs, check_vma=False)
```

```python
import math

import jax
import jax.numpy as jnp
import numpy as np
from jax import lax
from jax.experimental import pallas as pl
from jax.experimental.pallas import tpu as pltpu
from jax.sharding import PartitionSpec as P

NROT = 36
TAU = 1.0
GROUP = 32
STACK = 4
DEPTH = 2 * STACK
CLASSES = GROUP * STACK
LANES = 128
ROWS = 128
SHELLS = ROWS // 2
TAIL = 16
BAND = STACK * ROWS + TAIL
BATCH = 8
HIGH = lax.Precision.HIGHEST
F32 = jnp.float32
BF16 = jnp.bfloat16

HBM = pl.BlockSpec(memory_space=pltpu.HBM)
VMEM = pl.BlockSpec(memory_space=pltpu.VMEM)
SMEM = pl.BlockSpec(memory_space=pltpu.SMEM)


def rotation_steps():
    turns = np.arange(NROT)
    offset = turns * LANES // NROT
    fraction = ((turns * LANES) % NROT).astype(np.float32) / np.float32(NROT)
    keep = (np.float32(1.0) - fraction).astype(BF16).astype(np.float32)
    carry = fraction.astype(BF16).astype(np.float32)
    return offset, keep, carry


def lag_matrix():
    offset, keep, carry = rotation_steps()
    out = np.zeros((LANES, LANES), np.float32)
    for r in range(NROT):
        out[offset[r] % LANES, r] += keep[r]
        out[(offset[r] + 1) % LANES, r] += carry[r]
    return out


def rotation_matrices():
    offset, keep, carry = rotation_steps()
    out = np.zeros((NROT, LANES, LANES), np.float32)
    t = np.arange(LANES)
    for r in range(NROT):
        out[r, (t - offset[r]) % LANES, t] += keep[r]
        out[r, (t - offset[r] - 1) % LANES, t] += carry[r]
    return out.astype(BF16)


def contract(left, right, dims):
    return lax.dot_general(left, right, (dims, ((), ())), precision=HIGH, preferred_element_type=F32)


def weights_by_shell(group_row, table):
    groups, count = table.shape[1], group_row.shape[1]
    pick = (lax.broadcasted_iota(jnp.int32, (groups, count), 0) == group_row).astype(F32)
    return contract(table, pick, ((1,), (0,)))


def split_pair(value):
    high = value.astype(BF16).astype(F32)
    return jnp.concatenate([high, value - high], axis=1)


def join_pair(pair):
    return pair[:, : LANES // 2] + pair[:, LANES // 2 :]


def align(image, turn, rots):
    return jnp.dot(image, rots[turn], preferred_element_type=F32)


def keep_columns(by_shell, columns):
    for b in range(columns.shape[0]):
        columns[b, :, :BATCH] = by_shell[:, b * BATCH : (b + 1) * BATCH]


def slot_of(c):
    return (c // DEPTH) * 2 + c % 2, (c // 2) % STACK


def scale_rows(column, value):
    return jnp.concatenate([column * value[:SHELLS], column * value[SHELLS:]], axis=0)


def sums_kernel(assign, rotation, group, table, images, rotations, out, *scratch):
    classes, turns, assign_row, group_row, local, rows, rots, columns, sems = scratch
    count = rows.shape[0]
    moves = [
        (images, rows),
        (rotations, rots),
        (table, local),
        (group, group_row),
        (assign, assign_row),
        (assign, classes),
        (rotation, turns),
    ]
    copies = [pltpu.make_async_copy(source, target, sems.at[n]) for n, (source, target) in enumerate(moves)]
    for copy in copies:
        copy.start()
    for d in range(GROUP):
        out[d, : STACK * ROWS, :] = jnp.zeros((STACK * ROWS, LANES), BF16)
    for copy in copies[2:]:
        copy.wait()
    by_shell = weights_by_shell(group_row[...], local[...])
    keep_columns(by_shell, columns)
    n = lax.broadcasted_iota(jnp.int32, (CLASSES, count), 0)
    d, s = n // STACK, n % STACK
    member = ((d // 2) * DEPTH + s * 2 + d % 2 == assign_row[...]).astype(F32)
    pair = split_pair(contract(member, jnp.transpose(by_shell * by_shell), ((1,), (0,))))
    blank = jnp.zeros((TAIL - STACK, LANES), F32)
    for d in range(GROUP):
        tile = jnp.concatenate([pair[d * STACK : (d + 1) * STACK], blank], axis=0)
        out[d, STACK * ROWS :, :] = tile.astype(BF16)

    for copy in copies[:2]:
        copy.wait()

    def batch(b, _):
        weights = columns[b]
        for j in range(BATCH):
            i = b * BATCH + j
            d, s = slot_of(classes[0, i])
            turned = align(rows[i], turns[0, i], rots)
            at = pl.ds(pl.multiple_of(s * ROWS, ROWS), ROWS)
            held = out[d, at, :].astype(F32)
            out[d, at, :] = (held + scale_rows(weights[:, j : j + 1], turned)).astype(BF16)
        return 0

    lax.fori_loop(0, count // BATCH, batch, 0)


def class_sums(assign, rotation, group, table, images, rotations):
    count, groups = images.shape[0], table.shape[1]
    return pl.pallas_call(
        sums_kernel,
        out_shape=jax.ShapeDtypeStruct((GROUP, BAND, LANES), BF16),
        in_specs=[HBM] * 6,
        out_specs=VMEM,
        scratch_shapes=[
            pltpu.SMEM((1, count), jnp.int32),
            pltpu.SMEM((1, count), jnp.int32),
            pltpu.VMEM((1, count), jnp.int32),
            pltpu.VMEM((1, count), jnp.int32),
            pltpu.VMEM((SHELLS, groups), F32),
            pltpu.VMEM((count, ROWS, LANES), BF16),
            pltpu.VMEM((NROT, LANES, LANES), BF16),
            pltpu.VMEM((count // BATCH, SHELLS, LANES), F32),
            pltpu.SemaphoreType.DMA((7,)),
        ],
        compiler_params=pltpu.CompilerParams(vmem_limit_bytes=24 << 20),
        name="class_sums",
    )(assign, rotation, group, table, images, rotations)


def place_along_z():
    return lax.axis_index("cls") // 2 % STACK


def store_band(out, total):
    out[: STACK * ROWS, :] = total[: STACK * ROWS].astype(BF16)
    out[STACK * ROWS :, :] = split_pair(join_pair(total[STACK * ROWS :])).astype(BF16)


def group_kernel(bands, out):
    for at in range(0, STACK * ROWS, SHELLS):
        total = bands[0, at : at + SHELLS, :].astype(F32)
        for d in range(1, GROUP):
            total = total + bands[d, at : at + SHELLS, :].astype(F32)
        out[at : at + SHELLS, :] = total.astype(BF16)
    tail = jnp.sum(bands[:, STACK * ROWS :, :].astype(F32), axis=0)
    out[STACK * ROWS :, :] = split_pair(join_pair(tail)).astype(BF16)


def group_sums(bands):
    return pl.pallas_call(
        group_kernel,
        out_shape=jax.ShapeDtypeStruct((BAND, LANES), BF16),
        in_specs=[VMEM],
        out_specs=VMEM,
        compiler_params=pltpu.CompilerParams(vmem_limit_bytes=24 << 20),
        name="group_sums",
    )(bands)


def pair_kernel(mine, theirs, out):
    store_band(out, mine[...].astype(F32) + theirs[...].astype(F32))


def pair_sums(mine, theirs):
    return pl.pallas_call(
        pair_kernel,
        out_shape=jax.ShapeDtypeStruct((BAND, LANES), BF16),
        in_specs=[VMEM] * 2,
        out_specs=VMEM,
        compiler_params=pltpu.CompilerParams(vmem_limit_bytes=4 << 20),
        name="pair_sums",
    )(mine, theirs)


def average_kernel(mine, theirs, stack, own, tail):
    total = mine[...].astype(F32) + theirs[...].astype(F32)
    den = join_pair(total[STACK * ROWS :])
    tail[...] = split_pair(den).astype(BF16)
    for s in range(STACK):
        row = den[s : s + 1]
        column = jnp.transpose(jnp.broadcast_to(jnp.concatenate([row, row], axis=1), (LANES, LANES)))
        stack[s * ROWS : (s + 1) * ROWS, :] = (total[s * ROWS : (s + 1) * ROWS] / (column + TAU)).astype(BF16)
    own[...] = stack[pl.ds(pl.multiple_of(place_along_z() * ROWS, ROWS), ROWS), :]


def class_averages(mine, theirs):
    return pl.pallas_call(
        average_kernel,
        out_shape=(
            jax.ShapeDtypeStruct((STACK * ROWS, LANES), BF16),
            jax.ShapeDtypeStruct((ROWS, LANES), BF16),
            jax.ShapeDtypeStruct((TAIL, LANES), BF16),
        ),
        in_specs=[VMEM] * 2,
        out_specs=(VMEM, VMEM, VMEM),
        compiler_params=pltpu.CompilerParams(vmem_limit_bytes=4 << 20),
        name="class_averages",
    )(mine, theirs)


def copies_kernel(stack, tail, out):
    for at in range(0, STACK * ROWS, SHELLS):
        value = stack[at : at + SHELLS, :]
        for d in range(GROUP):
            out[d, at : at + SHELLS, :] = value
    value = tail[...]
    for d in range(GROUP):
        out[d, STACK * ROWS :, :] = value


def group_copies(stack, tail):
    return pl.pallas_call(
        copies_kernel,
        out_shape=jax.ShapeDtypeStruct((GROUP, BAND, LANES), BF16),
        in_specs=[VMEM] * 2,
        out_specs=VMEM,
        compiler_params=pltpu.CompilerParams(vmem_limit_bytes=24 << 20),
        name="group_copies",
    )(stack, tail)


def outputs_kernel(classes, turns, group_row, table, rows, rots, bands, lag_ref, resid, score, lever, *scratch):
    columns, held, out_sems, dens, lags, powers, energies = scratch
    count = rows.shape[0]
    by_shell = weights_by_shell(group_row[...], table[...])
    keep_columns(by_shell, columns)

    def leave(b):
        at = pl.ds(pl.multiple_of(b * BATCH, BATCH), BATCH)
        return pltpu.make_async_copy(held.at[at], resid.at[at], out_sems.at[b])

    def batch(b, _):
        weights = columns[b]
        for j in range(BATCH):
            i = b * BATCH + j
            d, s = slot_of(classes[0, i])
            image = rows[i]
            wide = image.astype(F32)
            turned = align(image, turns[0, i], rots)
            avg = bands[d, pl.ds(pl.multiple_of(s * ROWS, ROWS), ROWS), :].astype(F32)
            predicted = scale_rows(weights[:, j : j + 1], avg).astype(BF16)
            back = predicted.astype(F32)
            held[i] = (turned - back).astype(BF16)
            cross = lax.dot_general(image, predicted, (((0,), (0,)), ((), ())), preferred_element_type=F32)
            lag = cross[:8]
            for r in range(8, LANES, 8):
                lag = lag + pltpu.roll(cross[r : r + 8], LANES - r, 1)
            lags[pl.ds(pl.multiple_of(i * 8, 8), 8), :] = lag
            powers[pl.ds(i, 1), :] = jnp.sum(wide * wide, axis=0, keepdims=True)
            energies[pl.ds(i, 1), :] = jnp.sum(back * back, axis=0, keepdims=True)
            tile = bands[d, STACK * ROWS :, :].astype(F32)
            pick = lax.broadcasted_iota(jnp.int32, tile.shape, 0) == s
            dens[pl.ds(i, 1), :] = jnp.sum(jnp.where(pick, tile, 0.0), axis=0, keepdims=True)
        leave(b).start()
        return 0

    lax.fori_loop(0, count // BATCH, batch, 0)
    shift = lags[pl.ds(0, count, stride=8), :]
    for r in range(1, 8):
        shift = shift + pltpu.roll(lags[pl.ds(r, count, stride=8), :], LANES - r, 1)
    raw = contract(lag_ref[...], shift, ((0,), (1,)))
    pixels = ROWS * LANES
    power = jnp.sum(jnp.transpose(powers[...]), axis=0, keepdims=True)
    energy = jnp.sum(jnp.transpose(energies[...]), axis=0, keepdims=True)
    first = jnp.sqrt(power / pixels + 1e-05)
    second = jnp.sqrt(energy / pixels + 1e-05)
    score[...] = (raw / (math.sqrt(pixels) * first * second))[:NROT].astype(BF16)
    den = jnp.transpose(join_pair(dens[...]))
    lever[...] = (jnp.sum(by_shell * by_shell / (den + TAU), axis=0, keepdims=True) / SHELLS).astype(BF16)

    def finish(b, _):
        leave(b).wait()
        return 0

    lax.fori_loop(0, count // BATCH, finish, 0)


def particle_outputs(assign, rotation, group, table, images, rotations, bands):
    count = images.shape[0]
    per_particle = pltpu.VMEM((count, LANES), F32)
    return pl.pallas_call(
        outputs_kernel,
        out_shape=(
            jax.ShapeDtypeStruct(images.shape, BF16),
            jax.ShapeDtypeStruct((NROT, count), BF16),
            jax.ShapeDtypeStruct((1, count), BF16),
        ),
        in_specs=[SMEM] * 2 + [VMEM] * 6,
        out_specs=(HBM, VMEM, VMEM),
        scratch_shapes=[
            pltpu.VMEM((count // BATCH, SHELLS, LANES), F32),
            pltpu.VMEM((count, ROWS, LANES), BF16),
            pltpu.SemaphoreType.DMA((count // BATCH,)),
            per_particle,
            pltpu.VMEM((count * 8, LANES), F32),
            per_particle,
            per_particle,
        ],
        compiler_params=pltpu.CompilerParams(vmem_limit_bytes=24 << 20),
        name="particle_outputs",
    )(assign, rotation, group, table, images, rotations, bands, jnp.asarray(lag_matrix()))


def exchange(value):
    chips = np.arange(CLASSES).reshape(GROUP // 2, STACK, 2)
    groups = [chips[:, k, :].reshape(-1).tolist() for k in range(STACK)]
    return lax.all_to_all(value, "cls", split_axis=0, concat_axis=0, tiled=True, axis_index_groups=groups)


def swap_along_z(value, odd):
    def partner(chip):
        place = chip // 2 % STACK
        other = (place + (1 if place % 2 == odd else STACK - 1)) % STACK
        return chip + 2 * (other - place)

    return lax.ppermute(value, "cls", [(i, partner(i)) for i in range(CLASSES)])


def body(particles, assign, rotation, group, ctf):
    operands = (assign, rotation, group, ctf.T, particles[0], jnp.asarray(rotation_matrices()))
    pinned = [pltpu.with_memory_space_constraint(x, pltpu.HBM) for x in operands]
    band = group_sums(exchange(class_sums(*pinned)))
    band = pair_sums(band, swap_along_z(band, 0))
    stack, average, tail = class_averages(band, swap_along_z(band, 1))
    stack = lax.ppermute(stack, "half", [(0, 1), (1, 0)])
    bands = exchange(group_copies(stack, tail))
    residual, scores, leverage = particle_outputs(*operands, bands)
    return (average[None, None], residual[None], scores.T[None], leverage)


def solution(mesh):
    in_specs = (
        P("half", "cls", None, None),
        P("half", "cls"),
        P("half", "cls"),
        P("half", "cls"),
        P(),
    )
    out_specs = (
        P("half", "cls", None, None),
        P("half", "cls", None, None),
        P("half", "cls", None),
        P("half", "cls"),
    )
    return jax.shard_map(body, mesh=mesh, in_specs=in_specs, out_specs=out_specs, check_vma=False)
```

```python
import math

import jax
import jax.numpy as jnp
import numpy as np
from jax import lax
from jax.experimental import pallas as pl
from jax.experimental.pallas import tpu as pltpu
from jax.sharding import PartitionSpec as P

NROT = 36
TAU = 1.0
GROUP = 32
STACK = 4
DEPTH = 2 * STACK
CLASSES = GROUP * STACK
LANES = 128
ROWS = 128
SHELLS = ROWS // 2
TAIL = 16
BAND = STACK * ROWS + TAIL
BATCH = 8
HIGH = lax.Precision.HIGHEST
F32 = jnp.float32
BF16 = jnp.bfloat16

HBM = pl.BlockSpec(memory_space=pltpu.HBM)
VMEM = pl.BlockSpec(memory_space=pltpu.VMEM)
SMEM = pl.BlockSpec(memory_space=pltpu.SMEM)


def rotation_steps():
    turns = np.arange(NROT)
    offset = turns * LANES // NROT
    fraction = ((turns * LANES) % NROT).astype(np.float32) / np.float32(NROT)
    keep = (np.float32(1.0) - fraction).astype(BF16).astype(np.float32)
    carry = fraction.astype(BF16).astype(np.float32)
    return offset, keep, carry


def lag_matrix():
    offset, keep, carry = rotation_steps()
    out = np.zeros((LANES, LANES), np.float32)
    for r in range(NROT):
        out[offset[r] % LANES, r] += keep[r]
        out[(offset[r] + 1) % LANES, r] += carry[r]
    return out


def rotation_matrices():
    offset, keep, carry = rotation_steps()
    out = np.zeros((NROT, LANES, LANES), np.float32)
    t = np.arange(LANES)
    for r in range(NROT):
        out[r, (t - offset[r]) % LANES, t] += keep[r]
        out[r, (t - offset[r] - 1) % LANES, t] += carry[r]
    return out.astype(BF16)


def contract(left, right, dims):
    return lax.dot_general(left, right, (dims, ((), ())), precision=HIGH, preferred_element_type=F32)


def weights_by_shell(group_row, table):
    groups, count = table.shape[1], group_row.shape[1]
    pick = (lax.broadcasted_iota(jnp.int32, (groups, count), 0) == group_row).astype(F32)
    return contract(table, pick, ((1,), (0,)))


def split_pair(value):
    high = value.astype(BF16).astype(F32)
    return jnp.concatenate([high, value - high], axis=1)


def join_pair(pair):
    return pair[:, : LANES // 2] + pair[:, LANES // 2 :]


def align(image, turn, rots):
    return jnp.dot(image, rots[turn], preferred_element_type=F32)


def keep_columns(by_shell, columns):
    for b in range(columns.shape[0]):
        columns[b, :, :BATCH] = by_shell[:, b * BATCH : (b + 1) * BATCH]


def slot_of(c):
    return (c % 2) * (GROUP // 2) + c // DEPTH, (c // 2) % STACK


def scale_rows(column, value):
    return jnp.concatenate([column * value[:SHELLS], column * value[SHELLS:]], axis=0)


def sums_kernel(assign, rotation, group, table, images, rotations, out, *scratch):
    classes, turns, assign_row, group_row, local, rows, rots, columns, sems = scratch
    count = rows.shape[0]
    moves = [
        (images, rows),
        (rotations, rots),
        (table, local),
        (group, group_row),
        (assign, assign_row),
        (assign, classes),
        (rotation, turns),
    ]
    copies = [pltpu.make_async_copy(source, target, sems.at[n]) for n, (source, target) in enumerate(moves)]
    for copy in copies:
        copy.start()
    for d in range(GROUP):
        out[d, : STACK * ROWS, :] = jnp.zeros((STACK * ROWS, LANES), BF16)
    for copy in copies[2:]:
        copy.wait()
    by_shell = weights_by_shell(group_row[...], local[...])
    keep_columns(by_shell, columns)
    n = lax.broadcasted_iota(jnp.int32, (CLASSES, count), 0)
    d, s = n // STACK, n % STACK
    member = (d % (GROUP // 2) * DEPTH + s * 2 + d // (GROUP // 2) == assign_row[...]).astype(F32)
    pair = split_pair(contract(member, jnp.transpose(by_shell * by_shell), ((1,), (0,))))
    blank = jnp.zeros((TAIL - STACK, LANES), F32)
    for d in range(GROUP):
        tile = jnp.concatenate([pair[d * STACK : (d + 1) * STACK], blank], axis=0)
        out[d, STACK * ROWS :, :] = tile.astype(BF16)

    for copy in copies[:2]:
        copy.wait()

    def batch(b, _):
        weights = columns[b]
        for j in range(BATCH):
            i = b * BATCH + j
            d, s = slot_of(classes[0, i])
            turned = align(rows[i], turns[0, i], rots)
            at = pl.ds(pl.multiple_of(s * ROWS, ROWS), ROWS)
            held = out[d, at, :].astype(F32)
            out[d, at, :] = (held + scale_rows(weights[:, j : j + 1], turned)).astype(BF16)
        return 0

    lax.fori_loop(0, count // BATCH, batch, 0)


def class_sums(assign, rotation, group, table, images, rotations):
    count, groups = images.shape[0], table.shape[1]
    return pl.pallas_call(
        sums_kernel,
        out_shape=jax.ShapeDtypeStruct((GROUP, BAND, LANES), BF16),
        in_specs=[HBM] * 6,
        out_specs=VMEM,
        scratch_shapes=[
            pltpu.SMEM((1, count), jnp.int32),
            pltpu.SMEM((1, count), jnp.int32),
            pltpu.VMEM((1, count), jnp.int32),
            pltpu.VMEM((1, count), jnp.int32),
            pltpu.VMEM((SHELLS, groups), F32),
            pltpu.VMEM((count, ROWS, LANES), BF16),
            pltpu.VMEM((NROT, LANES, LANES), BF16),
            pltpu.VMEM((count // BATCH, SHELLS, LANES), F32),
            pltpu.SemaphoreType.DMA((7,)),
        ],
        compiler_params=pltpu.CompilerParams(vmem_limit_bytes=24 << 20),
        name="class_sums",
    )(assign, rotation, group, table, images, rotations)


def place_along_z():
    return lax.axis_index("cls") // 2 % STACK


def store_band(out, total):
    out[: STACK * ROWS, :] = total[: STACK * ROWS].astype(BF16)
    out[STACK * ROWS :, :] = split_pair(join_pair(total[STACK * ROWS :])).astype(BF16)


def group_kernel(bands, out):
    for at in range(0, STACK * ROWS, SHELLS):
        total = bands[0, at : at + SHELLS, :].astype(F32)
        for d in range(1, GROUP):
            total = total + bands[d, at : at + SHELLS, :].astype(F32)
        out[at : at + SHELLS, :] = total.astype(BF16)
    tail = jnp.sum(bands[:, STACK * ROWS :, :].astype(F32), axis=0)
    out[STACK * ROWS :, :] = split_pair(join_pair(tail)).astype(BF16)


def group_sums(bands):
    return pl.pallas_call(
        group_kernel,
        out_shape=jax.ShapeDtypeStruct((BAND, LANES), BF16),
        in_specs=[VMEM],
        out_specs=VMEM,
        compiler_params=pltpu.CompilerParams(vmem_limit_bytes=24 << 20),
        name="group_sums",
    )(bands)


def pair_kernel(mine, theirs, out):
    store_band(out, mine[...].astype(F32) + theirs[...].astype(F32))


def pair_sums(mine, theirs):
    return pl.pallas_call(
        pair_kernel,
        out_shape=jax.ShapeDtypeStruct((BAND, LANES), BF16),
        in_specs=[VMEM] * 2,
        out_specs=VMEM,
        compiler_params=pltpu.CompilerParams(vmem_limit_bytes=4 << 20),
        name="pair_sums",
    )(mine, theirs)


def average_kernel(mine, theirs, stack, own, tail):
    total = mine[...].astype(F32) + theirs[...].astype(F32)
    den = join_pair(total[STACK * ROWS :])
    tail[...] = split_pair(den).astype(BF16)
    for s in range(STACK):
        row = den[s : s + 1]
        column = jnp.transpose(jnp.broadcast_to(jnp.concatenate([row, row], axis=1), (LANES, LANES)))
        stack[s * ROWS : (s + 1) * ROWS, :] = (total[s * ROWS : (s + 1) * ROWS] / (column + TAU)).astype(BF16)
    own[...] = stack[pl.ds(pl.multiple_of(place_along_z() * ROWS, ROWS), ROWS), :]


def class_averages(mine, theirs):
    return pl.pallas_call(
        average_kernel,
        out_shape=(
            jax.ShapeDtypeStruct((STACK * ROWS, LANES), BF16),
            jax.ShapeDtypeStruct((ROWS, LANES), BF16),
            jax.ShapeDtypeStruct((TAIL, LANES), BF16),
        ),
        in_specs=[VMEM] * 2,
        out_specs=(VMEM, VMEM, VMEM),
        compiler_params=pltpu.CompilerParams(vmem_limit_bytes=4 << 20),
        name="class_averages",
    )(mine, theirs)


def copies_kernel(stack, tail, out):
    for at in range(0, STACK * ROWS, SHELLS):
        value = stack[at : at + SHELLS, :]
        for d in range(GROUP):
            out[d, at : at + SHELLS, :] = value
    value = tail[...]
    for d in range(GROUP):
        out[d, STACK * ROWS :, :] = value


def group_copies(stack, tail):
    return pl.pallas_call(
        copies_kernel,
        out_shape=jax.ShapeDtypeStruct((GROUP, BAND, LANES), BF16),
        in_specs=[VMEM] * 2,
        out_specs=VMEM,
        compiler_params=pltpu.CompilerParams(vmem_limit_bytes=24 << 20),
        name="group_copies",
    )(stack, tail)


def outputs_kernel(classes, turns, group_row, table, rows, rots, bands, lag_ref, resid, score, lever, *scratch):
    columns, held, out_sems, dens, lags, powers, energies = scratch
    count = rows.shape[0]
    by_shell = weights_by_shell(group_row[...], table[...])
    keep_columns(by_shell, columns)

    def leave(b):
        at = pl.ds(pl.multiple_of(b * BATCH, BATCH), BATCH)
        return pltpu.make_async_copy(held.at[at], resid.at[at], out_sems.at[b])

    def batch(b, _):
        weights = columns[b]
        for j in range(BATCH):
            i = b * BATCH + j
            d, s = slot_of(classes[0, i])
            image = rows[i]
            wide = image.astype(F32)
            turned = align(image, turns[0, i], rots)
            avg = bands[d, pl.ds(pl.multiple_of(s * ROWS, ROWS), ROWS), :].astype(F32)
            predicted = scale_rows(weights[:, j : j + 1], avg).astype(BF16)
            back = predicted.astype(F32)
            held[i] = (turned - back).astype(BF16)
            cross = lax.dot_general(image, predicted, (((0,), (0,)), ((), ())), preferred_element_type=F32)
            lag = cross[:8]
            for r in range(8, LANES, 8):
                lag = lag + pltpu.roll(cross[r : r + 8], LANES - r, 1)
            lags[pl.ds(pl.multiple_of(i * 8, 8), 8), :] = lag
            powers[pl.ds(i, 1), :] = jnp.sum(wide * wide, axis=0, keepdims=True)
            energies[pl.ds(i, 1), :] = jnp.sum(back * back, axis=0, keepdims=True)
            tile = bands[d, STACK * ROWS :, :].astype(F32)
            pick = lax.broadcasted_iota(jnp.int32, tile.shape, 0) == s
            dens[pl.ds(i, 1), :] = jnp.sum(jnp.where(pick, tile, 0.0), axis=0, keepdims=True)
        leave(b).start()
        return 0

    lax.fori_loop(0, count // BATCH, batch, 0)
    shift = lags[pl.ds(0, count, stride=8), :]
    for r in range(1, 8):
        shift = shift + pltpu.roll(lags[pl.ds(r, count, stride=8), :], LANES - r, 1)
    raw = contract(lag_ref[...], shift, ((0,), (1,)))
    pixels = ROWS * LANES
    power = jnp.sum(jnp.transpose(powers[...]), axis=0, keepdims=True)
    energy = jnp.sum(jnp.transpose(energies[...]), axis=0, keepdims=True)
    first = jnp.sqrt(power / pixels + 1e-05)
    second = jnp.sqrt(energy / pixels + 1e-05)
    score[...] = (raw / (math.sqrt(pixels) * first * second))[:NROT].astype(BF16)
    den = jnp.transpose(join_pair(dens[...]))
    lever[...] = (jnp.sum(by_shell * by_shell / (den + TAU), axis=0, keepdims=True) / SHELLS).astype(BF16)

    def finish(b, _):
        leave(b).wait()
        return 0

    lax.fori_loop(0, count // BATCH, finish, 0)


def particle_outputs(assign, rotation, group, table, images, rotations, bands):
    count = images.shape[0]
    per_particle = pltpu.VMEM((count, LANES), F32)
    return pl.pallas_call(
        outputs_kernel,
        out_shape=(
            jax.ShapeDtypeStruct(images.shape, BF16),
            jax.ShapeDtypeStruct((NROT, count), BF16),
            jax.ShapeDtypeStruct((1, count), BF16),
        ),
        in_specs=[SMEM] * 2 + [VMEM] * 6,
        out_specs=(HBM, VMEM, VMEM),
        scratch_shapes=[
            pltpu.VMEM((count // BATCH, SHELLS, LANES), F32),
            pltpu.VMEM((count, ROWS, LANES), BF16),
            pltpu.SemaphoreType.DMA((count // BATCH,)),
            per_particle,
            pltpu.VMEM((count * 8, LANES), F32),
            per_particle,
            per_particle,
        ],
        compiler_params=pltpu.CompilerParams(vmem_limit_bytes=24 << 20),
        name="particle_outputs",
    )(assign, rotation, group, table, images, rotations, bands, jnp.asarray(lag_matrix()))


def exchange(value):
    chips = np.arange(CLASSES).reshape(GROUP // 2, STACK, 2)
    groups = [chips[:, k, :].T.reshape(-1).tolist() for k in range(STACK)]
    return lax.all_to_all(value, "cls", split_axis=0, concat_axis=0, tiled=True, axis_index_groups=groups)


def swap_along_z(value, odd):
    def partner(chip):
        place = chip // 2 % STACK
        other = (place + (1 if place % 2 == odd else STACK - 1)) % STACK
        return chip + 2 * (other - place)

    return lax.ppermute(value, "cls", [(i, partner(i)) for i in range(CLASSES)])


def body(particles, assign, rotation, group, ctf):
    operands = (assign, rotation, group, ctf.T, particles[0], jnp.asarray(rotation_matrices()))
    pinned = [pltpu.with_memory_space_constraint(x, pltpu.HBM) for x in operands]
    band = group_sums(exchange(class_sums(*pinned)))
    band = pair_sums(band, swap_along_z(band, 0))
    stack, average, tail = class_averages(band, swap_along_z(band, 1))
    stack = lax.ppermute(stack, "half", [(0, 1), (1, 0)])
    bands = exchange(group_copies(stack, tail))
    residual, scores, leverage = particle_outputs(*operands, bands)
    return (average[None, None], residual[None], scores.T[None], leverage)


def solution(mesh):
    in_specs = (
        P("half", "cls", None, None),
        P("half", "cls"),
        P("half", "cls"),
        P("half", "cls"),
        P(),
    )
    out_specs = (
        P("half", "cls", None, None),
        P("half", "cls", None, None),
        P("half", "cls", None),
        P("half", "cls"),
    )
    return jax.shard_map(body, mesh=mesh, in_specs=in_specs, out_specs=out_specs, check_vma=False)
```

```python
import math

import jax
import jax.numpy as jnp
import numpy as np
from jax import lax
from jax.experimental import pallas as pl
from jax.experimental.pallas import tpu as pltpu
from jax.sharding import PartitionSpec as P

NROT = 36
TAU = 1.0
GROUP = 32
STACK = 4
DEPTH = 2 * STACK
CLASSES = GROUP * STACK
LANES = 128
ROWS = 128
SHELLS = ROWS // 2
TAIL = 8
BAND = STACK * ROWS + TAIL
BATCH = 8
HIGH = lax.Precision.HIGHEST
F32 = jnp.float32
BF16 = jnp.bfloat16

HBM = pl.BlockSpec(memory_space=pltpu.HBM)
VMEM = pl.BlockSpec(memory_space=pltpu.VMEM)
SMEM = pl.BlockSpec(memory_space=pltpu.SMEM)


def rotation_steps():
    turns = np.arange(NROT)
    offset = turns * LANES // NROT
    fraction = ((turns * LANES) % NROT).astype(np.float32) / np.float32(NROT)
    keep = (np.float32(1.0) - fraction).astype(BF16).astype(np.float32)
    carry = fraction.astype(BF16).astype(np.float32)
    return offset, keep, carry


def lag_matrix():
    offset, keep, carry = rotation_steps()
    out = np.zeros((LANES, LANES), np.float32)
    for r in range(NROT):
        out[offset[r] % LANES, r] += keep[r]
        out[(offset[r] + 1) % LANES, r] += carry[r]
    return out


def rotation_matrices():
    offset, keep, carry = rotation_steps()
    out = np.zeros((NROT, LANES, LANES), np.float32)
    t = np.arange(LANES)
    for r in range(NROT):
        out[r, (t - offset[r]) % LANES, t] += keep[r]
        out[r, (t - offset[r] - 1) % LANES, t] += carry[r]
    return out.astype(BF16)


def contract(left, right, dims):
    return lax.dot_general(left, right, (dims, ((), ())), precision=HIGH, preferred_element_type=F32)


def weights_by_shell(group_row, table):
    groups, count = table.shape[1], group_row.shape[1]
    pick = (lax.broadcasted_iota(jnp.int32, (groups, count), 0) == group_row).astype(F32)
    return contract(table, pick, ((1,), (0,)))


def split_pair(value):
    high = value.astype(BF16).astype(F32)
    return jnp.concatenate([high, value - high], axis=1)


def join_pair(pair):
    return pair[:, : LANES // 2] + pair[:, LANES // 2 :]


def align(image, turn, rots):
    return jnp.dot(image, rots[turn], preferred_element_type=F32)


def keep_columns(by_shell, columns):
    for b in range(columns.shape[0]):
        part = by_shell[:, b * BATCH : (b + 1) * BATCH]
        columns[b] = jnp.concatenate([part, jnp.zeros((SHELLS, LANES - BATCH), F32)], axis=1)


def slot_of(c):
    return (c % 2) * (GROUP // 2) + c // DEPTH, (c // 2) % STACK


def scale_rows(column, value):
    return jnp.concatenate([column * value[:SHELLS], column * value[SHELLS:]], axis=0)


def sums_kernel(assign, rotation, group, table, images, rotations, out, columns, weights_out, *scratch):
    classes, turns, assign_row, group_row, local, rows, rots, sems = scratch
    count = rows.shape[0]
    moves = [
        (images, rows),
        (rotations, rots),
        (table, local),
        (group, group_row),
        (assign, assign_row),
        (assign, classes),
        (rotation, turns),
    ]
    copies = [pltpu.make_async_copy(source, target, sems.at[n]) for n, (source, target) in enumerate(moves)]
    for copy in copies:
        copy.start()
    for d in range(GROUP):
        out[d, : STACK * ROWS, :] = jnp.zeros((STACK * ROWS, LANES), BF16)
    for copy in copies[2:]:
        copy.wait()
    by_shell = weights_by_shell(group_row[...], local[...])
    weights_out[...] = by_shell
    keep_columns(by_shell, columns)
    n = lax.broadcasted_iota(jnp.int32, (CLASSES, count), 0)
    d, s = n // STACK, n % STACK
    member = (d % (GROUP // 2) * DEPTH + s * 2 + d // (GROUP // 2) == assign_row[...]).astype(F32)
    pair = split_pair(contract(member, jnp.transpose(by_shell * by_shell), ((1,), (0,))))
    blank = jnp.zeros((TAIL - STACK, LANES), F32)
    for d in range(GROUP):
        tile = jnp.concatenate([pair[d * STACK : (d + 1) * STACK], blank], axis=0)
        out[d, STACK * ROWS :, :] = tile.astype(BF16)

    for copy in copies[:2]:
        copy.wait()

    def batch(b, _):
        weights = columns[b]
        for j in range(BATCH):
            i = b * BATCH + j
            d, s = slot_of(classes[0, i])
            turned = align(rows[i], turns[0, i], rots)
            at = pl.ds(pl.multiple_of(s * ROWS, ROWS), ROWS)
            held = out[d, at, :].astype(F32)
            out[d, at, :] = (held + scale_rows(weights[:, j : j + 1], turned)).astype(BF16)
        return 0

    lax.fori_loop(0, count // BATCH, batch, 0)


def class_sums(assign, rotation, group, table, images, rotations):
    count, groups = images.shape[0], table.shape[1]
    return pl.pallas_call(
        sums_kernel,
        out_shape=(
            jax.ShapeDtypeStruct((GROUP, BAND, LANES), BF16),
            jax.ShapeDtypeStruct((count // BATCH, SHELLS, LANES), F32),
            jax.ShapeDtypeStruct((SHELLS, count), F32),
        ),
        in_specs=[HBM] * 6,
        out_specs=(VMEM, VMEM, VMEM),
        scratch_shapes=[
            pltpu.SMEM((1, count), jnp.int32),
            pltpu.SMEM((1, count), jnp.int32),
            pltpu.VMEM((1, count), jnp.int32),
            pltpu.VMEM((1, count), jnp.int32),
            pltpu.VMEM((SHELLS, groups), F32),
            pltpu.VMEM((count, ROWS, LANES), BF16),
            pltpu.VMEM((NROT, LANES, LANES), BF16),
            pltpu.SemaphoreType.DMA((7,)),
        ],
        compiler_params=pltpu.CompilerParams(vmem_limit_bytes=24 << 20),
        name="class_sums",
    )(assign, rotation, group, table, images, rotations)


def place_along_z():
    return lax.axis_index("cls") // 2 % STACK


def store_band(out, total):
    out[: STACK * ROWS, :] = total[: STACK * ROWS].astype(BF16)
    out[STACK * ROWS :, :] = split_pair(join_pair(total[STACK * ROWS :])).astype(BF16)


def group_kernel(bands, out):
    for at in range(0, STACK * ROWS, SHELLS):
        total = bands[0, at : at + SHELLS, :].astype(F32)
        for d in range(1, GROUP):
            total = total + bands[d, at : at + SHELLS, :].astype(F32)
        out[at : at + SHELLS, :] = total.astype(BF16)
    tail = jnp.sum(bands[:, STACK * ROWS :, :].astype(F32), axis=0)
    out[STACK * ROWS :, :] = split_pair(join_pair(tail)).astype(BF16)


def group_sums(bands):
    return pl.pallas_call(
        group_kernel,
        out_shape=jax.ShapeDtypeStruct((BAND, LANES), BF16),
        in_specs=[VMEM],
        out_specs=VMEM,
        compiler_params=pltpu.CompilerParams(vmem_limit_bytes=24 << 20),
        name="group_sums",
    )(bands)


def pair_kernel(mine, theirs, out):
    store_band(out, mine[...].astype(F32) + theirs[...].astype(F32))


def pair_sums(mine, theirs):
    return pl.pallas_call(
        pair_kernel,
        out_shape=jax.ShapeDtypeStruct((BAND, LANES), BF16),
        in_specs=[VMEM] * 2,
        out_specs=VMEM,
        compiler_params=pltpu.CompilerParams(vmem_limit_bytes=4 << 20),
        name="pair_sums",
    )(mine, theirs)


def average_kernel(mine, theirs, stack, own, tail):
    total = mine[...].astype(F32) + theirs[...].astype(F32)
    den = join_pair(total[STACK * ROWS :])
    tail[...] = split_pair(den).astype(BF16)
    for s in range(STACK):
        row = den[s : s + 1]
        column = jnp.transpose(jnp.broadcast_to(jnp.concatenate([row, row], axis=1), (LANES, LANES)))
        stack[s * ROWS : (s + 1) * ROWS, :] = (total[s * ROWS : (s + 1) * ROWS] / (column + TAU)).astype(BF16)
    own[...] = stack[pl.ds(pl.multiple_of(place_along_z() * ROWS, ROWS), ROWS), :]


def class_averages(mine, theirs):
    return pl.pallas_call(
        average_kernel,
        out_shape=(
            jax.ShapeDtypeStruct((STACK * ROWS, LANES), BF16),
            jax.ShapeDtypeStruct((ROWS, LANES), BF16),
            jax.ShapeDtypeStruct((TAIL, LANES), BF16),
        ),
        in_specs=[VMEM] * 2,
        out_specs=(VMEM, VMEM, VMEM),
        compiler_params=pltpu.CompilerParams(vmem_limit_bytes=4 << 20),
        name="class_averages",
    )(mine, theirs)


def copies_kernel(stack, tail, out):
    for at in range(0, STACK * ROWS, SHELLS):
        value = stack[at : at + SHELLS, :]
        for d in range(GROUP):
            out[d, at : at + SHELLS, :] = value
    value = tail[...]
    for d in range(GROUP):
        out[d, STACK * ROWS :, :] = value


def group_copies(stack, tail):
    return pl.pallas_call(
        copies_kernel,
        out_shape=jax.ShapeDtypeStruct((GROUP, BAND, LANES), BF16),
        in_specs=[VMEM] * 2,
        out_specs=VMEM,
        compiler_params=pltpu.CompilerParams(vmem_limit_bytes=24 << 20),
        name="group_copies",
    )(stack, tail)


def outputs_kernel(classes, turns, columns, weights_in, rows, rots, bands, lag_ref, resid, score, lever, *scratch):
    held, out_sems, dens, lags, powers, energies = scratch
    count = rows.shape[0]
    by_shell = weights_in[...]

    def leave(b):
        at = pl.ds(pl.multiple_of(b * BATCH, BATCH), BATCH)
        return pltpu.make_async_copy(held.at[at], resid.at[at], out_sems.at[b])

    def batch(b, _):
        weights = columns[b]
        for j in range(BATCH):
            i = b * BATCH + j
            d, s = slot_of(classes[0, i])
            image = rows[i]
            wide = image.astype(F32)
            turned = align(image, turns[0, i], rots)
            avg = bands[d, pl.ds(pl.multiple_of(s * ROWS, ROWS), ROWS), :].astype(F32)
            predicted = scale_rows(weights[:, j : j + 1], avg).astype(BF16)
            back = predicted.astype(F32)
            held[i] = (turned - back).astype(BF16)
            cross = lax.dot_general(image, predicted, (((0,), (0,)), ((), ())), preferred_element_type=F32)
            lag = cross[:8]
            for r in range(8, LANES, 8):
                lag = lag + pltpu.roll(cross[r : r + 8], LANES - r, 1)
            lags[pl.ds(pl.multiple_of(i * 8, 8), 8), :] = lag
            powers[pl.ds(i, 1), :] = jnp.sum(wide * wide, axis=0, keepdims=True)
            energies[pl.ds(i, 1), :] = jnp.sum(back * back, axis=0, keepdims=True)
            tile = bands[d, STACK * ROWS :, :].astype(F32)
            pick = lax.broadcasted_iota(jnp.int32, tile.shape, 0) == s
            dens[pl.ds(i, 1), :] = jnp.sum(jnp.where(pick, tile, 0.0), axis=0, keepdims=True)
        leave(b).start()
        return 0

    lax.fori_loop(0, count // BATCH, batch, 0)
    shift = lags[pl.ds(0, count, stride=8), :]
    for r in range(1, 8):
        shift = shift + pltpu.roll(lags[pl.ds(r, count, stride=8), :], LANES - r, 1)
    raw = contract(lag_ref[...], shift, ((0,), (1,)))
    pixels = ROWS * LANES
    power = jnp.sum(jnp.transpose(powers[...]), axis=0, keepdims=True)
    energy = jnp.sum(jnp.transpose(energies[...]), axis=0, keepdims=True)
    first = jnp.sqrt(power / pixels + 1e-05)
    second = jnp.sqrt(energy / pixels + 1e-05)
    score[...] = (raw / (math.sqrt(pixels) * first * second))[:NROT].astype(BF16)
    den = jnp.transpose(join_pair(dens[...]))
    lever[...] = (jnp.sum(by_shell * by_shell / (den + TAU), axis=0, keepdims=True) / SHELLS).astype(BF16)

    def finish(b, _):
        leave(b).wait()
        return 0

    lax.fori_loop(0, count // BATCH, finish, 0)


def particle_outputs(assign, rotation, columns, weights, images, rotations, bands):
    count = images.shape[0]
    per_particle = pltpu.VMEM((count, LANES), F32)
    return pl.pallas_call(
        outputs_kernel,
        out_shape=(
            jax.ShapeDtypeStruct(images.shape, BF16),
            jax.ShapeDtypeStruct((NROT, count), BF16),
            jax.ShapeDtypeStruct((1, count), BF16),
        ),
        in_specs=[SMEM] * 2 + [VMEM] * 6,
        out_specs=(HBM, VMEM, VMEM),
        scratch_shapes=[
            pltpu.VMEM((count, ROWS, LANES), BF16),
            pltpu.SemaphoreType.DMA((count // BATCH,)),
            per_particle,
            pltpu.VMEM((count * 8, LANES), F32),
            per_particle,
            per_particle,
        ],
        compiler_params=pltpu.CompilerParams(vmem_limit_bytes=24 << 20),
        name="particle_outputs",
    )(assign, rotation, columns, weights, images, rotations, bands, jnp.asarray(lag_matrix()))


def exchange(value):
    chips = np.arange(CLASSES).reshape(GROUP // 2, STACK, 2)
    groups = [chips[:, k, :].T.reshape(-1).tolist() for k in range(STACK)]
    return lax.all_to_all(value, "cls", split_axis=0, concat_axis=0, tiled=True, axis_index_groups=groups)


def swap_along_z(value, odd):
    def partner(chip):
        place = chip // 2 % STACK
        other = (place + (1 if place % 2 == odd else STACK - 1)) % STACK
        return chip + 2 * (other - place)

    return lax.ppermute(value, "cls", [(i, partner(i)) for i in range(CLASSES)])


def body(particles, assign, rotation, group, ctf):
    images, rotations = particles[0], jnp.asarray(rotation_matrices())
    operands = (assign, rotation, group, ctf.T, images, rotations)
    pinned = [pltpu.with_memory_space_constraint(x, pltpu.HBM) for x in operands]
    bands, columns, weights = class_sums(*pinned)
    band = group_sums(exchange(bands))
    band = pair_sums(band, swap_along_z(band, 0))
    stack, average, tail = class_averages(band, swap_along_z(band, 1))
    stack = lax.ppermute(stack, "half", [(0, 1), (1, 0)])
    bands = exchange(group_copies(stack, tail))
    residual, scores, leverage = particle_outputs(assign, rotation, columns, weights, images, rotations, bands)
    return (average[None, None], residual[None], scores.T[None], leverage)


def solution(mesh):
    in_specs = (
        P("half", "cls", None, None),
        P("half", "cls"),
        P("half", "cls"),
        P("half", "cls"),
        P(),
    )
    out_specs = (
        P("half", "cls", None, None),
        P("half", "cls", None, None),
        P("half", "cls", None),
        P("half", "cls"),
    )
    return jax.shard_map(body, mesh=mesh, in_specs=in_specs, out_specs=out_specs, check_vma=False)
```

```python
import math

import jax
import jax.numpy as jnp
import numpy as np
from jax import lax
from jax.experimental import pallas as pl
from jax.experimental.pallas import tpu as pltpu
from jax.sharding import PartitionSpec as P

NROT = 36
TAU = 1.0
GROUP = 32
STACK = 4
DEPTH = 2 * STACK
CLASSES = GROUP * STACK
LANES = 128
ROWS = 128
SHELLS = ROWS // 2
TAIL = 8
BAND = STACK * ROWS + TAIL
BATCH = 8
HIGH = lax.Precision.HIGHEST
F32 = jnp.float32
BF16 = jnp.bfloat16

HBM = pl.BlockSpec(memory_space=pltpu.HBM)
VMEM = pl.BlockSpec(memory_space=pltpu.VMEM)
SMEM = pl.BlockSpec(memory_space=pltpu.SMEM)


def rotation_steps():
    turns = np.arange(NROT)
    offset = turns * LANES // NROT
    fraction = ((turns * LANES) % NROT).astype(np.float32) / np.float32(NROT)
    keep = (np.float32(1.0) - fraction).astype(BF16).astype(np.float32)
    carry = fraction.astype(BF16).astype(np.float32)
    return offset, keep, carry


def lag_matrix():
    offset, keep, carry = rotation_steps()
    out = np.zeros((LANES, LANES), np.float32)
    for r in range(NROT):
        out[offset[r] % LANES, r] += keep[r]
        out[(offset[r] + 1) % LANES, r] += carry[r]
    return out


def rotation_matrices():
    offset, keep, carry = rotation_steps()
    out = np.zeros((NROT, LANES, LANES), np.float32)
    t = np.arange(LANES)
    for r in range(NROT):
        out[r, (t - offset[r]) % LANES, t] += keep[r]
        out[r, (t - offset[r] - 1) % LANES, t] += carry[r]
    return out.astype(BF16)


def contract(left, right, dims):
    return lax.dot_general(left, right, (dims, ((), ())), precision=HIGH, preferred_element_type=F32)


def weights_by_shell(group_row, table):
    groups, count = table.shape[1], group_row.shape[1]
    pick = (lax.broadcasted_iota(jnp.int32, (groups, count), 0) == group_row).astype(F32)
    return contract(table, pick, ((1,), (0,)))


def split_pair(value):
    high = value.astype(BF16).astype(F32)
    return jnp.concatenate([high, value - high], axis=1)


def join_pair(pair):
    return pair[:, : LANES // 2] + pair[:, LANES // 2 :]


def align(image, turn, rots):
    return jnp.dot(image, rots[turn], preferred_element_type=F32)


def keep_columns(by_shell, columns):
    for b in range(columns.shape[0]):
        part = by_shell[:, b * BATCH : (b + 1) * BATCH]
        columns[b] = jnp.concatenate([part, jnp.zeros((SHELLS, LANES - BATCH), F32)], axis=1)


def slot_of(c):
    return (c % 2) * (GROUP // 2) + c // DEPTH, (c // 2) % STACK


def scale_rows(column, value):
    return jnp.concatenate([column * value[:SHELLS], column * value[SHELLS:]], axis=0)


def sums_kernel(assign, rotation, group, table, images, rotations, out, spread, weights_out, *scratch):
    classes, turns, assign_row, group_row, local, rows, rots, columns, sems = scratch
    count = rows.shape[0]
    moves = [
        (images, rows),
        (rotations, rots),
        (table, local),
        (group, group_row),
        (assign, assign_row),
        (assign, classes),
        (rotation, turns),
    ]
    copies = [pltpu.make_async_copy(source, target, sems.at[n]) for n, (source, target) in enumerate(moves)]
    for copy in copies:
        copy.start()
    for d in range(GROUP):
        out[d, : STACK * ROWS, :] = jnp.zeros((STACK * ROWS, LANES), BF16)
    for copy in copies[2:]:
        copy.wait()
    by_shell = weights_by_shell(group_row[...], local[...])
    weights_out[...] = by_shell
    keep_columns(by_shell, columns)
    n = lax.broadcasted_iota(jnp.int32, (CLASSES, count), 0)
    d, s = n // STACK, n % STACK
    member = (d % (GROUP // 2) * DEPTH + s * 2 + d // (GROUP // 2) == assign_row[...]).astype(F32)
    pair = split_pair(contract(member, jnp.transpose(by_shell * by_shell), ((1,), (0,))))
    blank = jnp.zeros((TAIL - STACK, LANES), F32)
    for d in range(GROUP):
        tile = jnp.concatenate([pair[d * STACK : (d + 1) * STACK], blank], axis=0)
        out[d, STACK * ROWS :, :] = tile.astype(BF16)

    for copy in copies[:2]:
        copy.wait()

    def batch(b, _):
        weights = columns[b]
        for j in range(BATCH):
            i = b * BATCH + j
            d, s = slot_of(classes[0, i])
            turned = align(rows[i], turns[0, i], rots)
            at = pl.ds(pl.multiple_of(s * ROWS, ROWS), ROWS)
            wide = jnp.broadcast_to(weights[:, j : j + 1], (SHELLS, LANES))
            spread[i] = wide
            held = out[d, at, :].astype(F32)
            out[d, at, :] = (held + scale_rows(wide, turned)).astype(BF16)
        return 0

    lax.fori_loop(0, count // BATCH, batch, 0)


def class_sums(assign, rotation, group, table, images, rotations):
    count, groups = images.shape[0], table.shape[1]
    return pl.pallas_call(
        sums_kernel,
        out_shape=(
            jax.ShapeDtypeStruct((GROUP, BAND, LANES), BF16),
            jax.ShapeDtypeStruct((count, SHELLS, LANES), F32),
            jax.ShapeDtypeStruct((SHELLS, count), F32),
        ),
        in_specs=[HBM] * 6,
        out_specs=(VMEM, VMEM, VMEM),
        scratch_shapes=[
            pltpu.SMEM((1, count), jnp.int32),
            pltpu.SMEM((1, count), jnp.int32),
            pltpu.VMEM((1, count), jnp.int32),
            pltpu.VMEM((1, count), jnp.int32),
            pltpu.VMEM((SHELLS, groups), F32),
            pltpu.VMEM((count, ROWS, LANES), BF16),
            pltpu.VMEM((NROT, LANES, LANES), BF16),
            pltpu.VMEM((count // BATCH, SHELLS, LANES), F32),
            pltpu.SemaphoreType.DMA((7,)),
        ],
        compiler_params=pltpu.CompilerParams(vmem_limit_bytes=24 << 20),
        name="class_sums",
    )(assign, rotation, group, table, images, rotations)


def place_along_z():
    return lax.axis_index("cls") // 2 % STACK


def store_band(out, total):
    out[: STACK * ROWS, :] = total[: STACK * ROWS].astype(BF16)
    out[STACK * ROWS :, :] = split_pair(join_pair(total[STACK * ROWS :])).astype(BF16)


def group_kernel(bands, out):
    for at in range(0, STACK * ROWS, SHELLS):
        total = bands[0, at : at + SHELLS, :].astype(F32)
        for d in range(1, GROUP):
            total = total + bands[d, at : at + SHELLS, :].astype(F32)
        out[at : at + SHELLS, :] = total.astype(BF16)
    tail = jnp.sum(bands[:, STACK * ROWS :, :].astype(F32), axis=0)
    out[STACK * ROWS :, :] = split_pair(join_pair(tail)).astype(BF16)


def group_sums(bands):
    return pl.pallas_call(
        group_kernel,
        out_shape=jax.ShapeDtypeStruct((BAND, LANES), BF16),
        in_specs=[VMEM],
        out_specs=VMEM,
        compiler_params=pltpu.CompilerParams(vmem_limit_bytes=24 << 20),
        name="group_sums",
    )(bands)


def pair_kernel(mine, theirs, out):
    store_band(out, mine[...].astype(F32) + theirs[...].astype(F32))


def pair_sums(mine, theirs):
    return pl.pallas_call(
        pair_kernel,
        out_shape=jax.ShapeDtypeStruct((BAND, LANES), BF16),
        in_specs=[VMEM] * 2,
        out_specs=VMEM,
        compiler_params=pltpu.CompilerParams(vmem_limit_bytes=4 << 20),
        name="pair_sums",
    )(mine, theirs)


def average_kernel(mine, theirs, stack, own, tail):
    total = mine[...].astype(F32) + theirs[...].astype(F32)
    den = join_pair(total[STACK * ROWS :])
    tail[...] = split_pair(den).astype(BF16)
    for s in range(STACK):
        row = den[s : s + 1]
        column = jnp.transpose(jnp.broadcast_to(jnp.concatenate([row, row], axis=1), (LANES, LANES)))
        stack[s * ROWS : (s + 1) * ROWS, :] = (total[s * ROWS : (s + 1) * ROWS] / (column + TAU)).astype(BF16)
    own[...] = stack[pl.ds(pl.multiple_of(place_along_z() * ROWS, ROWS), ROWS), :]


def class_averages(mine, theirs):
    return pl.pallas_call(
        average_kernel,
        out_shape=(
            jax.ShapeDtypeStruct((STACK * ROWS, LANES), BF16),
            jax.ShapeDtypeStruct((ROWS, LANES), BF16),
            jax.ShapeDtypeStruct((TAIL, LANES), BF16),
        ),
        in_specs=[VMEM] * 2,
        out_specs=(VMEM, VMEM, VMEM),
        compiler_params=pltpu.CompilerParams(vmem_limit_bytes=4 << 20),
        name="class_averages",
    )(mine, theirs)


def copies_kernel(stack, tail, out):
    for at in range(0, STACK * ROWS, SHELLS):
        value = stack[at : at + SHELLS, :]
        for d in range(GROUP):
            out[d, at : at + SHELLS, :] = value
    value = tail[...]
    for d in range(GROUP):
        out[d, STACK * ROWS :, :] = value


def group_copies(stack, tail):
    return pl.pallas_call(
        copies_kernel,
        out_shape=jax.ShapeDtypeStruct((GROUP, BAND, LANES), BF16),
        in_specs=[VMEM] * 2,
        out_specs=VMEM,
        compiler_params=pltpu.CompilerParams(vmem_limit_bytes=24 << 20),
        name="group_copies",
    )(stack, tail)


def eight_rows(value):
    return jnp.sum(value.reshape(value.shape[0] // 8, 8, LANES), axis=0)


def fold_rows(ref):
    count = ref.shape[0] // 8
    return sum(ref[pl.ds(r, count, stride=8), :] for r in range(8))


def outputs_kernel(classes, turns, spread, weights_in, rows, rots, bands, lag_ref, resid, score, lever, *scratch):
    held, out_sems, dens, lags, powers, energies = scratch
    count = rows.shape[0]
    by_shell = weights_in[...]

    def leave(b):
        at = pl.ds(pl.multiple_of(b * BATCH, BATCH), BATCH)
        return pltpu.make_async_copy(held.at[at], resid.at[at], out_sems.at[b])

    def batch(b, _):
        for j in range(BATCH):
            i = b * BATCH + j
            d, s = slot_of(classes[0, i])
            image = rows[i]
            wide = image.astype(F32)
            turned = align(image, turns[0, i], rots)
            avg = bands[d, pl.ds(pl.multiple_of(s * ROWS, ROWS), ROWS), :].astype(F32)
            predicted = scale_rows(spread[i], avg).astype(BF16)
            back = predicted.astype(F32)
            held[i] = (turned - back).astype(BF16)
            cross = lax.dot_general(image, predicted, (((0,), (0,)), ((), ())), preferred_element_type=F32)
            lag = cross[:8]
            for r in range(8, LANES, 8):
                lag = lag + pltpu.roll(cross[r : r + 8], LANES - r, 1)
            at = pl.ds(pl.multiple_of(i * 8, 8), 8)
            lags[at, :] = lag
            powers[at, :] = eight_rows(wide * wide)
            energies[at, :] = eight_rows(back * back)
            tile = bands[d, STACK * ROWS :, :].astype(F32)
            pick = lax.broadcasted_iota(jnp.int32, tile.shape, 0) == s
            dens[at, :] = jnp.where(pick, tile, 0.0)
        leave(b).start()
        return 0

    lax.fori_loop(0, count // BATCH, batch, 0)
    shift = lags[pl.ds(0, count, stride=8), :]
    for r in range(1, 8):
        shift = shift + pltpu.roll(lags[pl.ds(r, count, stride=8), :], LANES - r, 1)
    raw = contract(lag_ref[...], shift, ((0,), (1,)))
    pixels = ROWS * LANES
    power = jnp.sum(jnp.transpose(fold_rows(powers)), axis=0, keepdims=True)
    energy = jnp.sum(jnp.transpose(fold_rows(energies)), axis=0, keepdims=True)
    first = jnp.sqrt(power / pixels + 1e-05)
    second = jnp.sqrt(energy / pixels + 1e-05)
    score[...] = (raw / (math.sqrt(pixels) * first * second))[:NROT].astype(BF16)
    den = jnp.transpose(join_pair(fold_rows(dens)))
    lever[...] = (jnp.sum(by_shell * by_shell / (den + TAU), axis=0, keepdims=True) / SHELLS).astype(BF16)

    def finish(b, _):
        leave(b).wait()
        return 0

    lax.fori_loop(0, count // BATCH, finish, 0)


def particle_outputs(assign, rotation, spread, weights, images, rotations, bands):
    count = images.shape[0]
    per_particle = pltpu.VMEM((count * 8, LANES), F32)
    return pl.pallas_call(
        outputs_kernel,
        out_shape=(
            jax.ShapeDtypeStruct(images.shape, BF16),
            jax.ShapeDtypeStruct((NROT, count), BF16),
            jax.ShapeDtypeStruct((1, count), BF16),
        ),
        in_specs=[SMEM] * 2 + [VMEM] * 6,
        out_specs=(HBM, VMEM, VMEM),
        scratch_shapes=[
            pltpu.VMEM((count, ROWS, LANES), BF16),
            pltpu.SemaphoreType.DMA((count // BATCH,)),
            per_particle,
            per_particle,
            per_particle,
            per_particle,
        ],
        compiler_params=pltpu.CompilerParams(vmem_limit_bytes=24 << 20),
        name="particle_outputs",
    )(assign, rotation, spread, weights, images, rotations, bands, jnp.asarray(lag_matrix()))


def exchange(value):
    chips = np.arange(CLASSES).reshape(GROUP // 2, STACK, 2)
    groups = [chips[:, k, :].T.reshape(-1).tolist() for k in range(STACK)]
    return lax.all_to_all(value, "cls", split_axis=0, concat_axis=0, tiled=True, axis_index_groups=groups)


def swap_along_z(value, odd):
    def partner(chip):
        place = chip // 2 % STACK
        other = (place + (1 if place % 2 == odd else STACK - 1)) % STACK
        return chip + 2 * (other - place)

    return lax.ppermute(value, "cls", [(i, partner(i)) for i in range(CLASSES)])


def body(particles, assign, rotation, group, ctf):
    images, rotations = particles[0], jnp.asarray(rotation_matrices())
    operands = (assign, rotation, group, ctf.T, images, rotations)
    pinned = [pltpu.with_memory_space_constraint(x, pltpu.HBM) for x in operands]
    bands, spread, weights = class_sums(*pinned)
    band = group_sums(exchange(bands))
    band = pair_sums(band, swap_along_z(band, 0))
    stack, average, tail = class_averages(band, swap_along_z(band, 1))
    stack = lax.ppermute(stack, "half", [(0, 1), (1, 0)])
    bands = exchange(group_copies(stack, tail))
    residual, scores, leverage = particle_outputs(assign, rotation, spread, weights, images, rotations, bands)
    return (average[None, None], residual[None], scores.T[None], leverage)


def solution(mesh):
    in_specs = (
        P("half", "cls", None, None),
        P("half", "cls"),
        P("half", "cls"),
        P("half", "cls"),
        P(),
    )
    out_specs = (
        P("half", "cls", None, None),
        P("half", "cls", None, None),
        P("half", "cls", None),
        P("half", "cls"),
    )
    return jax.shard_map(body, mesh=mesh, in_specs=in_specs, out_specs=out_specs, check_vma=False)
```

```python
import math

import jax
import jax.numpy as jnp
import numpy as np
from jax import lax
from jax.experimental import pallas as pl
from jax.experimental.pallas import tpu as pltpu
from jax.sharding import PartitionSpec as P

NROT = 36
TAU = 1.0
GROUP = 32
STACK = 4
DEPTH = 2 * STACK
CLASSES = GROUP * STACK
LANES = 128
ROWS = 128
SHELLS = ROWS // 2
TAIL = 8
BAND = STACK * ROWS + TAIL
BATCH = 8
HIGH = lax.Precision.HIGHEST
F32 = jnp.float32
BF16 = jnp.bfloat16

HBM = pl.BlockSpec(memory_space=pltpu.HBM)
VMEM = pl.BlockSpec(memory_space=pltpu.VMEM)
SMEM = pl.BlockSpec(memory_space=pltpu.SMEM)


def rotation_steps():
    turns = np.arange(NROT)
    offset = turns * LANES // NROT
    fraction = ((turns * LANES) % NROT).astype(np.float32) / np.float32(NROT)
    keep = (np.float32(1.0) - fraction).astype(BF16).astype(np.float32)
    carry = fraction.astype(BF16).astype(np.float32)
    return offset, keep, carry


def lag_matrix():
    offset, keep, carry = rotation_steps()
    out = np.zeros((LANES, LANES), np.float32)
    for r in range(NROT):
        out[offset[r] % LANES, r] += keep[r]
        out[(offset[r] + 1) % LANES, r] += carry[r]
    return out


def rotation_matrices():
    offset, keep, carry = rotation_steps()
    out = np.zeros((NROT, LANES, LANES), np.float32)
    t = np.arange(LANES)
    for r in range(NROT):
        out[r, (t - offset[r]) % LANES, t] += keep[r]
        out[r, (t - offset[r] - 1) % LANES, t] += carry[r]
    return out.astype(BF16)


def contract(left, right, dims):
    return lax.dot_general(left, right, (dims, ((), ())), precision=HIGH, preferred_element_type=F32)


def weights_by_shell(group_row, table):
    groups, count = table.shape[1], group_row.shape[1]
    pick = (lax.broadcasted_iota(jnp.int32, (groups, count), 0) == group_row).astype(F32)
    return contract(table, pick, ((1,), (0,)))


def split_pair(value):
    high = value.astype(BF16).astype(F32)
    return jnp.concatenate([high, value - high], axis=1)


def join_pair(pair):
    return pair[:, : LANES // 2] + pair[:, LANES // 2 :]


def align(image, turn, rots):
    return jnp.dot(image, rots[turn], preferred_element_type=F32)


def keep_columns(by_shell, columns):
    for b in range(columns.shape[0]):
        part = by_shell[:, b * BATCH : (b + 1) * BATCH]
        columns[b] = jnp.concatenate([part, jnp.zeros((SHELLS, LANES - BATCH), F32)], axis=1)


def slot_of(c):
    return (c % 2) * (GROUP // 2) + c // DEPTH, (c // 2) % STACK


def scale_rows(column, value):
    return jnp.concatenate([column * value[:SHELLS], column * value[SHELLS:]], axis=0)


def sums_kernel(assign, rotation, group, table, images, rotations, out, spread, weights_out, *scratch):
    classes, turns, assign_row, group_row, local, rows, rots, columns, sems = scratch
    count = rows.shape[0]
    moves = [
        (images, rows),
        (rotations, rots),
        (table, local),
        (group, group_row),
        (assign, assign_row),
        (assign, classes),
        (rotation, turns),
    ]
    copies = [pltpu.make_async_copy(source, target, sems.at[n]) for n, (source, target) in enumerate(moves)]
    for copy in copies:
        copy.start()
    for d in range(GROUP):
        out[d, : STACK * ROWS, :] = jnp.zeros((STACK * ROWS, LANES), BF16)
    for copy in copies[2:]:
        copy.wait()
    by_shell = weights_by_shell(group_row[...], local[...])
    weights_out[...] = by_shell
    keep_columns(by_shell, columns)
    n = lax.broadcasted_iota(jnp.int32, (CLASSES, count), 0)
    d, s = n // STACK, n % STACK
    member = (d % (GROUP // 2) * DEPTH + s * 2 + d // (GROUP // 2) == assign_row[...]).astype(F32)
    pair = split_pair(contract(member, jnp.transpose(by_shell * by_shell), ((1,), (0,))))
    blank = jnp.zeros((TAIL - STACK, LANES), F32)
    for d in range(GROUP):
        tile = jnp.concatenate([pair[d * STACK : (d + 1) * STACK], blank], axis=0)
        out[d, STACK * ROWS :, :] = tile.astype(BF16)

    for copy in copies[:2]:
        copy.wait()

    def batch(b, _):
        weights = columns[b]
        for j in range(BATCH):
            i = b * BATCH + j
            d, s = slot_of(classes[0, i])
            turned = align(rows[i], turns[0, i], rots)
            at = pl.ds(pl.multiple_of(s * ROWS, ROWS), ROWS)
            wide = jnp.broadcast_to(weights[:, j : j + 1], (SHELLS, LANES))
            spread[i] = wide
            held = out[d, at, :].astype(F32)
            out[d, at, :] = (held + scale_rows(wide, turned)).astype(BF16)
        return 0

    lax.fori_loop(0, count // BATCH, batch, 0)


def class_sums(assign, rotation, group, table, images, rotations):
    count, groups = images.shape[0], table.shape[1]
    return pl.pallas_call(
        sums_kernel,
        out_shape=(
            jax.ShapeDtypeStruct((GROUP, BAND, LANES), BF16),
            jax.ShapeDtypeStruct((count, SHELLS, LANES), F32),
            jax.ShapeDtypeStruct((SHELLS, count), F32),
        ),
        in_specs=[HBM] * 6,
        out_specs=(VMEM, VMEM, VMEM),
        scratch_shapes=[
            pltpu.SMEM((1, count), jnp.int32),
            pltpu.SMEM((1, count), jnp.int32),
            pltpu.VMEM((1, count), jnp.int32),
            pltpu.VMEM((1, count), jnp.int32),
            pltpu.VMEM((SHELLS, groups), F32),
            pltpu.VMEM((count, ROWS, LANES), BF16),
            pltpu.VMEM((NROT, LANES, LANES), BF16),
            pltpu.VMEM((count // BATCH, SHELLS, LANES), F32),
            pltpu.SemaphoreType.DMA((7,)),
        ],
        compiler_params=pltpu.CompilerParams(vmem_limit_bytes=24 << 20),
        name="class_sums",
    )(assign, rotation, group, table, images, rotations)


def place_along_z():
    return lax.axis_index("cls") // 2 % STACK


def store_band(out, total):
    out[: STACK * ROWS, :] = total[: STACK * ROWS].astype(BF16)
    out[STACK * ROWS :, :] = split_pair(join_pair(total[STACK * ROWS :])).astype(BF16)


def group_kernel(bands, out):
    for at in range(0, STACK * ROWS, SHELLS):
        total = bands[0, at : at + SHELLS, :].astype(F32)
        for d in range(1, GROUP):
            total = total + bands[d, at : at + SHELLS, :].astype(F32)
        out[at : at + SHELLS, :] = total.astype(BF16)
    tail = jnp.sum(bands[:, STACK * ROWS :, :].astype(F32), axis=0)
    out[STACK * ROWS :, :] = split_pair(join_pair(tail)).astype(BF16)


def group_sums(bands):
    return pl.pallas_call(
        group_kernel,
        out_shape=jax.ShapeDtypeStruct((BAND, LANES), BF16),
        in_specs=[VMEM],
        out_specs=VMEM,
        compiler_params=pltpu.CompilerParams(vmem_limit_bytes=24 << 20),
        name="group_sums",
    )(bands)


def pair_kernel(mine, theirs, out):
    store_band(out, mine[...].astype(F32) + theirs[...].astype(F32))


def pair_sums(mine, theirs):
    return pl.pallas_call(
        pair_kernel,
        out_shape=jax.ShapeDtypeStruct((BAND, LANES), BF16),
        in_specs=[VMEM] * 2,
        out_specs=VMEM,
        compiler_params=pltpu.CompilerParams(vmem_limit_bytes=4 << 20),
        name="pair_sums",
    )(mine, theirs)


def average_kernel(mine, theirs, stack, own, tail):
    total = mine[...].astype(F32) + theirs[...].astype(F32)
    den = join_pair(total[STACK * ROWS :])
    tail[...] = split_pair(den).astype(BF16)
    for s in range(STACK):
        row = den[s : s + 1]
        column = jnp.transpose(jnp.broadcast_to(jnp.concatenate([row, row], axis=1), (LANES, LANES)))
        stack[s * ROWS : (s + 1) * ROWS, :] = (total[s * ROWS : (s + 1) * ROWS] / (column + TAU)).astype(BF16)
    own[...] = stack[pl.ds(pl.multiple_of(place_along_z() * ROWS, ROWS), ROWS), :]


def class_averages(mine, theirs):
    return pl.pallas_call(
        average_kernel,
        out_shape=(
            jax.ShapeDtypeStruct((STACK * ROWS, LANES), BF16),
            jax.ShapeDtypeStruct((ROWS, LANES), BF16),
            jax.ShapeDtypeStruct((TAIL, LANES), BF16),
        ),
        in_specs=[VMEM] * 2,
        out_specs=(VMEM, VMEM, VMEM),
        compiler_params=pltpu.CompilerParams(vmem_limit_bytes=4 << 20),
        name="class_averages",
    )(mine, theirs)


def copies_kernel(stack, tail, out):
    for at in range(0, STACK * ROWS, SHELLS):
        value = stack[at : at + SHELLS, :]
        for d in range(GROUP):
            out[d, at : at + SHELLS, :] = value
    value = tail[...]
    for d in range(GROUP):
        out[d, STACK * ROWS :, :] = value


def group_copies(stack, tail):
    return pl.pallas_call(
        copies_kernel,
        out_shape=jax.ShapeDtypeStruct((GROUP, BAND, LANES), BF16),
        in_specs=[VMEM] * 2,
        out_specs=VMEM,
        compiler_params=pltpu.CompilerParams(vmem_limit_bytes=24 << 20),
        name="group_copies",
    )(stack, tail)


def eight_rows(value):
    return jnp.sum(value.reshape(value.shape[0] // 8, 8, LANES), axis=0)


def fold_rows(ref):
    count = ref.shape[0] // 8
    return sum(ref[pl.ds(r, count, stride=8), :] for r in range(8))


def outputs_kernel(classes, turns, spread, weights_in, rows, rots, bands, lag_ref, resid, score, lever, *scratch):
    held, out_sems, dens, lags, powers, energies = scratch
    count = rows.shape[0]
    by_shell = weights_in[...]

    def leave(b):
        at = pl.ds(pl.multiple_of(b * BATCH, BATCH), BATCH)
        return pltpu.make_async_copy(held.at[at], resid.at[at], out_sems.at[b])

    def batch(b, _):
        for j in range(BATCH):
            i = b * BATCH + j
            d, s = slot_of(classes[0, i])
            image = rows[i]
            wide = image.astype(F32)
            turned = align(image, turns[0, i], rots)
            avg = bands[d, pl.ds(pl.multiple_of(s * ROWS, ROWS), ROWS), :].astype(F32)
            predicted = scale_rows(spread[i], avg).astype(BF16)
            back = predicted.astype(F32)
            held[i] = (turned - back).astype(BF16)
            cross = lax.dot_general(image, predicted, (((0,), (0,)), ((), ())), preferred_element_type=F32)
            lag = cross[:8]
            for r in range(8, LANES, 8):
                lag = lag + pltpu.roll(cross[r : r + 8], LANES - r, 1)
            at = pl.ds(pl.multiple_of(i * 8, 8), 8)
            lags[at, :] = lag
            powers[at, :] = eight_rows(wide * wide)
            energies[at, :] = eight_rows(back * back)
            tile = bands[d, STACK * ROWS :, :].astype(F32)
            pick = lax.broadcasted_iota(jnp.int32, tile.shape, 0) == s
            dens[at, :] = jnp.where(pick, tile, 0.0)
        leave(b).start()
        return 0

    lax.fori_loop(0, count // BATCH, batch, 0)
    shift = lags[pl.ds(0, count, stride=8), :]
    for r in range(1, 8):
        shift = shift + pltpu.roll(lags[pl.ds(r, count, stride=8), :], LANES - r, 1)
    raw = contract(lag_ref[...], shift, ((0,), (1,)))
    pixels = ROWS * LANES
    power = jnp.sum(jnp.transpose(fold_rows(powers)), axis=0, keepdims=True)
    energy = jnp.sum(jnp.transpose(fold_rows(energies)), axis=0, keepdims=True)
    first = jnp.sqrt(power / pixels + 1e-05)
    second = jnp.sqrt(energy / pixels + 1e-05)
    score[...] = (raw / (math.sqrt(pixels) * first * second))[:NROT].astype(BF16)
    den = jnp.transpose(join_pair(fold_rows(dens)))
    lever[...] = (jnp.sum(by_shell * by_shell / (den + TAU), axis=0, keepdims=True) / SHELLS).astype(BF16)

    def finish(b, _):
        leave(b).wait()
        return 0

    lax.fori_loop(0, count // BATCH, finish, 0)


def particle_outputs(assign, rotation, spread, weights, images, rotations, bands):
    count = images.shape[0]
    per_particle = pltpu.VMEM((count * 8, LANES), F32)
    return pl.pallas_call(
        outputs_kernel,
        out_shape=(
            jax.ShapeDtypeStruct(images.shape, BF16),
            jax.ShapeDtypeStruct((NROT, count), BF16),
            jax.ShapeDtypeStruct((1, count), BF16),
        ),
        in_specs=[SMEM] * 2 + [VMEM] * 6,
        out_specs=(HBM, VMEM, VMEM),
        scratch_shapes=[
            pltpu.VMEM((count, ROWS, LANES), BF16),
            pltpu.SemaphoreType.DMA((count // BATCH,)),
            per_particle,
            per_particle,
            per_particle,
            per_particle,
        ],
        compiler_params=pltpu.CompilerParams(vmem_limit_bytes=24 << 20),
        name="particle_outputs",
    )(assign, rotation, spread, weights, images, rotations, bands, jnp.asarray(lag_matrix()))


def exchange(value):
    chips = np.arange(CLASSES).reshape(GROUP // 2, STACK, 2)
    groups = [chips[:, k, :].T.reshape(-1).tolist() for k in range(STACK)]
    return lax.all_to_all(value, "cls", split_axis=0, concat_axis=0, tiled=True, axis_index_groups=groups)


def swap_along_z(value, odd):
    def partner(chip):
        place = chip // 2 % STACK
        other = (place + (1 if place % 2 == odd else STACK - 1)) % STACK
        return chip + 2 * (other - place)

    return lax.ppermute(value, "cls", [(i, partner(i)) for i in range(CLASSES)])


def body(particles, assign, rotation, group, ctf):
    images, rotations = particles[0], jnp.asarray(rotation_matrices())
    operands = (assign, rotation, group, ctf.T, images, rotations)
    pinned = [pltpu.with_memory_space_constraint(x, pltpu.HBM) for x in operands]
    bands, spread, weights = class_sums(*pinned)
    band = group_sums(exchange(bands))
    band = pair_sums(band, swap_along_z(band, 1))
    stack, average, tail = class_averages(band, swap_along_z(band, 0))
    stack = lax.ppermute(stack, "half", [(0, 1), (1, 0)])
    bands = exchange(group_copies(stack, tail))
    residual, scores, leverage = particle_outputs(assign, rotation, spread, weights, images, rotations, bands)
    return (average[None, None], residual[None], scores.T[None], leverage)


def solution(mesh):
    in_specs = (
        P("half", "cls", None, None),
        P("half", "cls"),
        P("half", "cls"),
        P("half", "cls"),
        P(),
    )
    out_specs = (
        P("half", "cls", None, None),
        P("half", "cls", None, None),
        P("half", "cls", None),
        P("half", "cls"),
    )
    return jax.shard_map(body, mesh=mesh, in_specs=in_specs, out_specs=out_specs, check_vma=False)
```
